32 devices in a mesh: gx: 4 (over z), gy: 4 (over x, core), gz: 2 (over y).
Axes of the slice: x: 2, y: 2, z: 4, core: 2. Of those that a mesh axis runs over, the one named last changes fastest.
Arguments:
- populations: float32 [19, 32, 32, 256], P(None, 'gx', 'gy', 'gz'), as said below
- solid: int32 [32, 32, 256], P('gx', 'gy', 'gz'), may hold values 0 or 1
- marker_pos: float32 [256, 3, 128], P(('gx', 'gy', 'gz')), may hold values from 2 to 125, as said below
- anchor_offset: float32 [256, 3, 128], P(('gx', 'gy', 'gz')), may hold values from -3 to 3
- links: int32 [256, 2, 128], P(('gx', 'gy', 'gz')), may hold values from 0 to 127
- patch_col: int32 [256, 1], P(('gx', 'gy', 'gz')), may hold values from 0 to 3; in each aligned block of 8 rows (0 to 7, 8 to 15, ...) at most 4 rows name the same one
Outputs:
- new_populations: float32 [19, 32, 32, 256], P(None, 'gx', 'gy', 'gz')
- marker_shift: float32 [256, 3, 128], P(('gx', 'gy', 'gz'))
The draws below stay inside these ranges and needn't reach their ends.
Inputs may be any that keep to these rules, and one draw needn't show every extreme that they name: `marker_pos`: each marker lies from 2 to 5 cells along the first coordinate of its patch, 2 to 5 along the second, 2 to 125 along the third. `patch_col`: among the 8 blocks of one device no patch index is named more than 4 times. `populations`: every population is positive.
All inputs are finite; a program needn't handle non-finite values. No bound on the sum of `solid` on one device may be relied on, other than what follows from the above.
Results may differ from the reference program's by a relative error of at most 0.00035.
Values sent between devices are 32-bit elements; how exact they have to be, the bound alone decides.
A program may use at most 64 MiB of HBM per device.

```python
import math
import jax
import jax.numpy as jnp
import numpy as np

CX = 8
CY = 8
CZ = 128
BLK_DEV = 8
MARK = 128
STEPS = 3
CAP = 4
NX = 32
NY = 32
NZ = 256
NBLK = 256
N_GX = 4
N_GY = 4
N_GZ = 2


WEIGHTS = (1.0 / 3.0,) + (1.0 / 18.0,) * 6 + (1.0 / 36.0,) * 12


def draw_populations(key, part):
    shape = (19, NX, NY, NZ)
    relative = 1.0 + 0.12 * jnp.clip(jax.random.normal(key, shape, jnp.float32), -2.5, 2.5)
    return relative * jnp.array(WEIGHTS, jnp.float32)[:, None, None, None]


def draw_marker_pos(key, part):
    fraction = jax.random.uniform(key, (NBLK, 3, MARK), jnp.float32)
    span = jnp.array([CX - 5, CY - 5, CZ - 5], jnp.float32)[None, :, None]
    return 2.0 + fraction * span


def touch_ends(values, key, smallest, top_value):
    shape = values.shape
    place = [jax.random.randint(jax.random.fold_in(key, axis), (), 0, shape[axis]) for axis in range(len(shape))]
    values = values.at[tuple(place)].set(smallest)
    longest = shape.index(max(shape))
    place[longest] = (place[longest] + 1) % shape[longest]
    return values.at[tuple(place)].set(top_value)


def level_of(stream_key, shape, shards, least, largest):
    factor_of = 1.0
    for position, shards_of in shards:
        steps = jax.random.uniform(jax.random.fold_in(jax.random.fold_in(stream_key, 6), position), (shards_of,), jnp.float32, least / len(shards), largest / len(shards))
        factor_of = factor_of * jnp.repeat(jnp.exp(steps), shape[position] // shards_of).reshape((-1,) + (1,) * (len(shape) - 1 - position))
    return factor_of


def routed_block(stream_key, own, number, rows, amount, top, bound, lean):
    order = jax.random.permutation(stream_key, amount)
    heavy_load, common = portions_of(amount, rows * top, bound, lean, True), portions_of(amount, rows * top, bound, lean, False)
    places = jnp.arange(amount)

    def named(sizes, turn):
        used = int((sizes > 0).sum())
        fixed = max(1, used // 4)
        passed = fixed + (places - fixed + turn * (used - fixed)) % max(1, amount - fixed)
        return jnp.zeros((amount,), jnp.int32).at[order[jnp.where(places < fixed, places, passed)]].set(jnp.asarray(sizes, jnp.int32))

    sizes = jnp.where(number % 4 == 0, named(heavy_load, number // 4), named(common, number - number // 4 - 1))
    mixed = jax.random.permutation(jax.random.fold_in(own, 3), amount)
    giver, taker = mixed[0:amount // 2 * 2:2], mixed[1:amount // 2 * 2:2]
    room = jnp.minimum(sizes[giver] - 1, bound - sizes[taker]) // 2
    room = jnp.where((giver == order[0]) | (taker == order[0]) | (sizes[taker] == 0), 0, jnp.maximum(room, 0))
    passed = jax.random.randint(jax.random.fold_in(own, 4), (amount // 2,), 0, 1 << 20) % (room + 1)
    sizes = sizes.at[giver].add(-passed).at[taker].add(passed)
    members = jnp.searchsorted(jnp.cumsum(sizes), jnp.arange(rows * top), side="right").astype(jnp.int32)
    grid = members.reshape(top, rows).T
    grid = grid[jax.random.permutation(jax.random.fold_in(own, 1), rows)]
    turn = jax.random.randint(jax.random.fold_in(own, 2), (rows, 1), 0, top)
    return jnp.take_along_axis(grid, (jnp.arange(top)[None, :] + turn) % top, axis=1)


def portions_of(amount, total, limit, slope, full):
    portions = [(1 << 20) // math.isqrt(rank ** slope) + 1 for rank in range(1, amount + 1)]
    largest = limit if full else min(limit, max(-(-total // amount), total * portions[0] // sum(portions)))
    least = 1 if total - largest >= amount - 1 else 0
    counts, spare = [largest] + [least] * (amount - 1), total - largest - least * (amount - 1)
    while spare > 0:
        free = [i for i in range(1, amount) if counts[i] < largest] or [i for i in range(1, amount) if counts[i] < limit]
        whole, left = sum([portions[i] for i in free]), spare
        for i in free:
            more = min(limit - counts[i], max(1, left * portions[i] // whole), spare)
            counts[i] = counts[i] + more
            spare = spare - more
    return np.array(counts)


def scatter_about(key, extent, scale, most, shards=(), kind=jnp.bfloat16):
    values = scale * jax.random.normal(key, extent, jnp.float32)
    if shards:
        values = values * level_of(key, extent, shards, -0.22, 0.18)
    return jnp.clip(values, -most, most).astype(kind)


def setup_inputs(seed: int = 0) -> dict:
    streams_of = jax.random.split(jax.random.key(seed), 7)
    populations = draw_populations(jax.random.fold_in(streams_of[6], 71), 0)
    solid = touch_ends((jax.random.randint(streams_of[1], (NX, NY, NZ), 0, 10) < 1).astype(jnp.int32), jax.random.fold_in(streams_of[1], 1), 0, 1)
    marker_pos = draw_marker_pos(jax.random.fold_in(streams_of[6], 71), 0)
    anchor_offset = scatter_about(streams_of[3], (NBLK, 3, MARK), 1.0, 3.0, ((0, 32),), jnp.float32)
    links = touch_ends(jax.random.randint(streams_of[4], (NBLK, 2, MARK), 0, MARK), jax.random.fold_in(streams_of[4], 1), 0, MARK - 1).astype(jnp.int32)
    patch_col_keys = jax.random.split(jax.random.fold_in(streams_of[5], 1), NBLK // BLK_DEV)
    patch_col_turns = jax.random.permutation(jax.random.fold_in(streams_of[5], 3), NBLK // BLK_DEV)
    patch_col = jax.vmap(lambda own, number: routed_block(jax.random.fold_in(streams_of[5], 2), own, number, BLK_DEV, N_GX, 1, CAP, 2))(patch_col_keys, patch_col_turns).reshape((NBLK, 1))
    return dict(populations=populations, solid=solid, marker_pos=marker_pos, anchor_offset=anchor_offset, links=links, patch_col=patch_col)


VELOCITY = ((0, 0, 0), (1, 0, 0), (-1, 0, 0), (0, 1, 0), (0, -1, 0), (0, 0, 1), (0, 0, -1),
            (1, 1, 0), (-1, -1, 0), (1, -1, 0), (-1, 1, 0), (1, 0, 1), (-1, 0, -1), (1, 0, -1), (-1, 0, 1),
            (0, 1, 1), (0, -1, -1), (0, 1, -1), (0, -1, 1))
WEIGHTS = (1.0 / 3.0,) + (1.0 / 18.0,) * 6 + (1.0 / 36.0,) * 12
OPPOSITE = (0, 2, 1, 4, 3, 6, 5, 8, 7, 10, 9, 12, 11, 14, 13, 16, 15, 18, 17)
TAU = 0.8
K_TETHER = 0.05
K_SPRING = 0.1


def project(vector, direction):
    total = None
    for column in range(3):
        if direction[column] != 0:
            term = vector[column] if direction[column] == 1 else -vector[column]
            total = term if total is None else total + term
    if total is None:
        total = jnp.zeros_like(vector[0])
    return total


def moments(parts):
    density = parts[0]
    for number in range(1, 19):
        density = density + parts[number]
    momentum = []
    for column in range(3):
        total = jnp.zeros_like(density)
        for number in range(19):
            sign = VELOCITY[number][column]
            if sign == 1:
                total = total + parts[number]
            elif sign == -1:
                total = total - parts[number]
        momentum.append(total)
    return density, momentum


def collide(parts, field, solid):
    density, momentum = moments(parts)
    speed = [(momentum[column] + 0.5 * field[column]) / density for column in range(3)]
    square = speed[0] * speed[0] + speed[1] * speed[1] + speed[2] * speed[2]
    power = speed[0] * field[0] + speed[1] * field[1] + speed[2] * field[2]
    factor = 1.0 - 0.5 / TAU
    walls = solid == 1
    result = []
    for number in range(19):
        along = project(speed, VELOCITY[number])
        pushed = project(field, VELOCITY[number])
        balance = WEIGHTS[number] * density * (1.0 + 3.0 * along + 4.5 * along * along - 1.5 * square)
        source = factor * WEIGHTS[number] * (3.0 * (pushed - power) + 9.0 * along * pushed)
        post = parts[number] - (parts[number] - balance) / TAU + source
        result.append(jnp.where(walls, parts[OPPOSITE[number]], post))
    return jnp.stack(result)


def marker_force(current, rest, anchor, links):
    total = K_TETHER * (anchor - current)
    for column in range(2):
        chosen = jnp.broadcast_to(links[:, column:column + 1, :], current.shape)
        total = total + K_SPRING * ((jnp.take_along_axis(current, chosen, axis=2) - current)
                                    - (jnp.take_along_axis(rest, chosen, axis=2) - rest))
    return total


def corner_table(current, corners):
    floors = jnp.floor(current)
    base = floors.astype(jnp.int32)
    per_dim = []
    for dim in range(3):
        coord = current[:, dim, :]
        lowest = floors[:, dim, :]
        options = []
        for offset in range(2):
            weight = jnp.maximum(0.0, 1.0 - jnp.abs(coord - (lowest + offset)))
            cell = base[:, dim, :] + offset + corners[dim][:, None]
            options.append((cell.reshape(-1), weight.reshape(-1)))
        per_dim.append(options)
    table = []
    for first in per_dim[0]:
        for second in per_dim[1]:
            for third in per_dim[2]:
                table.append((first[0], second[0], third[0], first[1] * second[1] * third[1]))
    return table


def reference(populations, solid, marker_pos, anchor_offset, links, patch_col):
    blocks = jnp.arange(NBLK, dtype=jnp.int32)
    owner = blocks // BLK_DEV
    corner_x = (patch_col[:, 0] * CX).astype(jnp.int32)
    corner_y = (((owner // N_GZ) % N_GY) * CY).astype(jnp.int32)
    corner_z = ((owner % N_GZ) * CZ).astype(jnp.int32)
    corners = (corner_x, corner_y, corner_z)
    anchor = marker_pos + anchor_offset
    current = marker_pos
    parts = populations
    for repeat in range(STEPS):
        force = marker_force(current, marker_pos, anchor, links)
        table = corner_table(current, corners)
        flat_force = jnp.transpose(force, (1, 0, 2)).reshape(3, -1)
        field = jnp.zeros((3, NX, NY, NZ), jnp.float32)
        for cell_x, cell_y, cell_z, weight in table:
            field = field.at[:, cell_x, cell_y, cell_z].add(flat_force * weight[None, :])
        post = collide(parts, field, solid)
        parts = jnp.stack([jnp.roll(post[number], shift=VELOCITY[number], axis=(0, 1, 2)) for number in range(19)])
        density, momentum = moments(parts)
        velocity = jnp.stack([momentum[column] / density for column in range(3)])
        motion = jnp.zeros((3, NBLK * MARK), jnp.float32)
        for cell_x, cell_y, cell_z, weight in table:
            motion = motion + velocity[:, cell_x, cell_y, cell_z] * weight[None, :]
        current = current + jnp.transpose(motion.reshape(3, NBLK, MARK), (1, 0, 2))
    return parts, current - marker_pos
```

```python
import functools

import jax
import jax.numpy as jnp
from jax import lax
from jax.experimental import pallas as pl
from jax.experimental.pallas import tpu as pltpu
from jax.sharding import PartitionSpec as P

STEPS = 3
VELOCITY = (
    (0, 0, 0), (1, 0, 0), (-1, 0, 0), (0, 1, 0), (0, -1, 0), (0, 0, 1), (0, 0, -1),
    (1, 1, 0), (-1, -1, 0), (1, -1, 0), (-1, 1, 0), (1, 0, 1), (-1, 0, -1), (1, 0, -1),
    (-1, 0, 1), (0, 1, 1), (0, -1, -1), (0, 1, -1), (0, -1, 1),
)
WEIGHTS = (1.0 / 3.0,) + (1.0 / 18.0,) * 6 + (1.0 / 36.0,) * 12
OPPOSITE = (0, 2, 1, 4, 3, 6, 5, 8, 7, 10, 9, 12, 11, 14, 13, 16, 15, 18, 17)
TAU = 0.8
K_TETHER = 0.05
K_SPRING = 0.1
NUMBER = {c: q for q, c in enumerate(VELOCITY)}
ORDER = (
    [q for q in range(19) if VELOCITY[q][0] == 0]
    + [q for q in range(19) if VELOCITY[q][0] == 1]
    + [q for q in range(19) if VELOCITY[q][0] == -1]
)
PLACE = {q: i for i, q in enumerate(ORDER)}
Y_MOVERS = [
    [NUMBER[(0, s, 0)], NUMBER[(1, s, 0)], NUMBER[(-1, s, 0)], NUMBER[(0, s, 1)], NUMBER[(0, s, -1)]]
    for s in (1, -1)
]
Z_MOVERS = [
    [NUMBER[(0, 0, s)], NUMBER[(1, 0, s)], NUMBER[(-1, 0, s)], NUMBER[(0, 1, s)], NUMBER[(0, -1, s)]]
    for s in (1, -1)
]
MESH = pl.DeviceIdType.MESH
PARK = -1000.0
SPREAD_UNROLL = 16
CELL_UNROLL = 8
WIDE = 1024
HALF = 64


def axis_sum(values, column):
    total = None
    for q in range(19):
        sign = VELOCITY[q][column]
        if sign == 0:
            continue
        term = values[q]
        total = (term if sign == 1 else -term) if total is None else (
            total + term if sign == 1 else total - term
        )
    return total


def moments(f):
    density = f[0]
    for q in range(1, 19):
        density = density + f[q]
    return density, [axis_sum(f, column) for column in range(3)]


def project(vector, direction):
    total = None
    for column in range(3):
        if direction[column]:
            term = vector[column] if direction[column] == 1 else -vector[column]
            total = term if total is None else total + term
    return total


def collide(f, density, momentum, field, wall):
    over = 1.0 / density
    omega = 1.0 / TAU
    factor = 1.0 - 0.5 / TAU
    if field is None:
        u = [momentum[k] * over for k in range(3)]
    else:
        u = [(momentum[k] + 0.5 * field[k]) * over for k in range(3)]
    square = u[0] * u[0] + u[1] * u[1] + u[2] * u[2]
    base = omega * density * (1.0 - 1.5 * square)
    if field is not None:
        power = u[0] * field[0] + u[1] * field[1] + u[2] * field[2]
        base = base - (3.0 * factor) * power
    scaled = omega * density
    post = [None] * 19
    rest = (1.0 - omega) * f[0] + WEIGHTS[0] * base
    post[0] = jnp.where(wall, f[0], rest)
    for q in range(1, 19, 2):
        p = OPPOSITE[q]
        along = project(u, VELOCITY[q])
        flow = scaled * along
        inner = 4.5 * flow
        odd = 3.0 * flow
        if field is not None:
            pushed = project(field, VELOCITY[q])
            inner = inner + (9.0 * factor) * pushed
            odd = odd + (3.0 * factor) * pushed
        even = WEIGHTS[q] * (base + along * inner)
        odd = WEIGHTS[q] * odd
        post[q] = jnp.where(wall, f[p], (1.0 - omega) * f[q] + (even + odd))
        post[p] = jnp.where(wall, f[q], (1.0 - omega) * f[p] + (even - odd))
    return post


def kernel(
    sizes,
    pop_hbm, solid_hbm, mpos_hbm, moff_hbm, links_hbm, pcol_hbm,
    outf, outs,
    pop, solid, mpos, moff, links, pcol,
    post, ysend, yhalo, zsend, zhalo, zin, mom, gfield, vfield,
    vedge, vmid, pull,
    msend, mrecv, disp, dsend, dback, where_to, edge_terms, mid_terms, pz, edge_plane, mid_plane,
    in_sem, msend_sem, mrecv_sem, hsend_sem, hrecv_sem, bsend_sem, brecv_sem,
):
    nx, ny, nz, blocks, cap, cx = sizes
    slots = nx * cap
    gx, gy, gz = lax.axis_index("gx"), lax.axis_index("gy"), lax.axis_index("gz")
    right, left = lax.rem(gx + 1, nx), lax.rem(gx + nx - 1, nx)
    up, down = lax.rem(gy + 1, ny), lax.rem(gy + ny - 1, ny)
    other = lax.rem(gz + 1, nz)

    def fetch(source, target, n):
        copy = pltpu.make_async_copy(source, target, in_sem.at[n])
        copy.start()
        return copy

    small = [
        fetch(source, target, n)
        for n, (source, target) in enumerate(
            ((pcol_hbm, pcol), (mpos_hbm, mpos), (moff_hbm, moff), (links_hbm, links))
        )
    ]
    barrier = pltpu.get_barrier_semaphore()
    near = [(a, b, gz) for a in (right, left) for b in (up, down)]
    near += [(right, gy, other), (left, gy, other)]
    for o in range(1, nx):
        near.append((lax.rem(gx + o, nx), gy, gz))
    near += [(gx, up, other), (gx, down, other), (gx, up, gz), (gx, down, gz), (gx, gy, other)]
    for device in near:
        pl.semaphore_signal(barrier, inc=1, device_id=device, device_id_type=MESH)
    rims = [
        fetch(pop_hbm.at[:, pl.ds(0, 1)], pop.at[:, pl.ds(0, 1)], 4),
        fetch(pop_hbm.at[:, pl.ds(cx - 1, 1)], pop.at[:, pl.ds(cx - 1, 1)], 5),
        fetch(solid_hbm, solid, 6),
    ]
    core = fetch(pop_hbm.at[:, pl.ds(1, cx - 2)], pop.at[:, pl.ds(1, cx - 2)], 7)

    row = lax.broadcasted_iota(jnp.int32, (8, 128), 0)
    lane = lax.broadcasted_iota(jnp.int32, (8, 128), 1)

    for copy in small:
        copy.wait()
    named = [jnp.broadcast_to(pcol[:, b : b + 1], (8, 128)) for b in range(blocks)]
    spots = []
    for b in range(blocks):
        spot = named[b] * cap
        for e in range(b):
            spot = spot + jnp.where(named[e] == named[b], 1, 0)
        spots.append(spot)
        where_to[b] = spot
    tiles = []
    for b in range(blocks):
        tiles.append(
            jnp.concatenate(
                [mpos[k, b : b + 1, :] for k in range(3)]
                + [moff[k, b : b + 1, :] for k in range(3)]
                + [links[b].astype(jnp.float32)],
                axis=0,
            )
        )
    empty = jnp.where(row < 3, PARK, 0.0)
    for s in range(slots):
        tile = empty
        for b in range(blocks):
            tile = jnp.where(spots[b] == s, tiles[b], tile)
        msend[s] = tile

    pl.semaphore_wait(barrier, len(near))

    def exchange(source, target, count, send_sem, recv_sem):
        copies = []
        for o in range(1, nx):
            to = lax.rem(gx + o, nx)
            copy = pltpu.make_async_remote_copy(
                src_ref=source.at[pl.ds(to * count, count)],
                dst_ref=target.at[pl.ds(gx * count, count)],
                send_sem=send_sem.at[o],
                recv_sem=recv_sem.at[o],
                device_id=(to, gy, gz),
                device_id_type=MESH,
            )
            copy.start()
            copies.append(copy)
        for k in range(count):
            target[gx * count + k] = source[gx * count + k]
        return copies

    marker_copies = exchange(msend, mrecv, cap, msend_sem, mrecv_sem)

    def sender(step, base):
        copies = []

        def go(source, target, device):
            n = base + len(copies)
            copy = pltpu.make_async_remote_copy(
                src_ref=source,
                dst_ref=target,
                send_sem=hsend_sem.at[step, n],
                recv_sem=hrecv_sem.at[step, n],
                device_id=device,
                device_id_type=MESH,
            )
            copy.start()
            copies.append(copy)

        return go, copies

    def halo_x(step):
        go, copies = sender(step, 0)
        for d, b in ((0, up), (1, down)):
            for j, x, a in ((1, cx - 1, right), (2, 0, left)):
                go(
                    ysend.at[step, d, j, pl.ds(x, 1)],
                    yhalo.at[step, d, j, pl.ds(cx, 1)],
                    (a, b, gz),
                )
        z = zsend.at[step, 0]
        go(z, zhalo.at[step, 1], (right, gy, other))
        go(z, zhalo.at[step, 2], (left, gy, other))
        go(post.at[step, pl.ds(9, 5), cx], post.at[step, pl.ds(9, 5), 0], (right, gy, gz))
        go(post.at[step, pl.ds(14, 5), 1], post.at[step, pl.ds(14, 5), cx + 1], (left, gy, gz))
        return copies

    def halo_yz(step):
        go, copies = sender(step, 8)
        z = zsend.at[step, 1]
        go(z, zhalo.at[step, 3], (gx, up, other))
        go(z, zhalo.at[step, 4], (gx, down, other))
        go(ysend.at[step, 0], yhalo.at[step, 0, :, pl.ds(0, cx)], (gx, up, gz))
        go(ysend.at[step, 1], yhalo.at[step, 1, :, pl.ds(0, cx)], (gx, down, gz))
        go(z, zhalo.at[step, 0], (gx, gy, other))
        return copies

    def over_edges(body, carry):
        return lax.fori_loop(0, 2, lambda i, c: body(i * (cx - 1), c), carry, unroll=2)

    def over_middle(body, carry):
        return lax.fori_loop(1, cx - 1, body, carry, unroll=cx - 2)

    def emit(step, x, values):
        for q in range(19):
            post[step, PLACE[q], x + 1] = values[q]

    def rim(step, x, values, packed):
        for d, edge in ((0, 7), (1, 0)):
            for j, q in enumerate(Y_MOVERS[d]):
                ysend[step, d, j, pl.ds(x, 1)] = values[q][edge : edge + 1, :]
        for d, edge in ((0, 127), (1, 0)):
            for j, q in enumerate(Z_MOVERS[d]):
                column = jnp.broadcast_to(values[q][:, edge : edge + 1], (8, 128))
                packed = jnp.where(lane == x + (d * HALF + j * 8), column, packed)
        return packed

    def stream(step, x):
        turned = pltpu.roll(zin[...], lax.rem(128 - x, 128), axis=1)
        f = []
        for q in range(19):
            c = VELOCITY[q]
            tile = post[step, PLACE[q], x + 1 - c[0]]
            if c[1]:
                d = 0 if c[1] == 1 else 1
                j = Y_MOVERS[d].index(q)
                if c[0] == 1:
                    at = lax.rem(x + cx, cx + 1)
                else:
                    at = x - c[0]
                line = jnp.broadcast_to(yhalo[step, d, j, pl.ds(at, 1)], (8, 128))
                tile = jnp.where(row == (0 if d == 0 else 7), line, pltpu.roll(tile, 1 if d == 0 else 7, axis=0))
            if c[2]:
                d = 0 if c[2] == 1 else 1
                j = Z_MOVERS[d].index(q)
                k = d * HALF + j * 8
                column = jnp.broadcast_to(turned[:, k : k + 1], (8, 128))
                tile = jnp.where(
                    lane == (0 if d == 0 else 127), column, pltpu.roll(tile, 1 if d == 0 else 127, axis=1)
                )
            f.append(tile)
            outf[q, x] = tile
        density, momentum = moments(f)
        mom[0, x] = density
        over = 1.0 / density
        for k in range(3):
            mom[k + 1, x] = momentum[k]
            vfield[k, x] = momentum[k] * over

    def combine(step, whole):
        face = zhalo[step, 0]
        group = lax.rem(lane, HALF) // 8
        inside = lax.rem(lane, 8)
        forward = pltpu.roll(face, 1, axis=1)
        backward = pltpu.roll(face, 127, axis=1)
        if whole:
            forward = jnp.where(inside == 0, pltpu.roll(zhalo[step, 1], 121, axis=1), forward)
            backward = jnp.where(inside == 7, pltpu.roll(zhalo[step, 2], 7, axis=1), backward)
        rising = jnp.where(
            row == 0, pltpu.roll(zhalo[step, 3], 1, axis=0), pltpu.roll(face, 1, axis=0)
        )
        falling = jnp.where(
            row == 7, pltpu.roll(zhalo[step, 4], 7, axis=0), pltpu.roll(face, 7, axis=0)
        )
        zin[...] = jnp.where(
            group == 0,
            face,
            jnp.where(
                group == 1,
                forward,
                jnp.where(group == 2, backward, jnp.where(group == 3, rising, falling)),
            ),
        )

    edges = (0, cx - 1)
    middle = tuple(range(1, cx - 1))
    inner = tuple(range(2, cx - 2))

    def spread(step, xs, fresh, terms, plane):
        size = len(xs) * 8
        n = 3 * size
        depth = lax.broadcasted_iota(jnp.int32, (128, 128), 0).astype(jnp.float32)
        cell = row.astype(jnp.float32)

        def one(s, carry):
            info = mrecv[s]
            if step == 0:
                shift = jnp.zeros((8, 128), jnp.float32)
                disp[s] = shift
            else:
                shift = disp[s]
            position = info + shift
            at = pl.ds(pl.multiple_of(s * 128, 128), 128)
            if fresh:
                rest_to_anchor = pltpu.roll(info, 5, axis=0)
                force = K_TETHER * ((info + rest_to_anchor) - position)
                if step > 0:
                    for k in range(2):
                        index = jnp.broadcast_to(info[6 + k : 7 + k, :], (8, 128)).astype(jnp.int32)
                        chosen = jnp.take_along_axis(shift, index, axis=1)
                        force = force + K_SPRING * (chosen - shift)
                    pull[s] = force
                wz = jnp.maximum(0.0, 1.0 - jnp.abs(position[2:3, :] - depth))
                high = wz.astype(jnp.bfloat16)
                pz[0:128, at] = high
                pz[128:256, at] = (wz - high.astype(jnp.float32)).astype(jnp.bfloat16)
            else:
                force = pull[s]
            wx = jnp.maximum(0.0, 1.0 - jnp.abs(position[0:1, :] - cell))
            wy = jnp.maximum(0.0, 1.0 - jnp.abs(position[1:2, :] - cell))
            full = jnp.concatenate([wx[i : i + 1, :] * wy for i in xs], axis=0)
            plane[0:size, at] = full
            for k in range(3):
                term = force[k : k + 1, :] * full
                high = term.astype(jnp.bfloat16)
                terms[k * size : k * size + size, at] = high
                terms[n + k * size : n + k * size + size, at] = (
                    term - high.astype(jnp.float32)
                ).astype(jnp.bfloat16)
            return carry

        lax.fori_loop(0, slots, one, 0, unroll=SPREAD_UNROLL)
        product = lax.dot_general(
            terms[0 : 2 * n], pz[...], (((1,), (1,)), ((), ())), preferred_element_type=jnp.float32
        )
        total = product[0:n, 0:128] + (product[0:n, 128:256] + product[n : 2 * n, 0:128])
        for k in range(3):
            for i, x in enumerate(xs):
                gfield[k, x] = total[k * size + i * 8 : k * size + i * 8 + 8]

    def sample(xs, vsplit, plane):
        size = len(xs) * 8
        n = 3 * size
        v = jnp.concatenate([vfield[k, x] for k in range(3) for x in xs], axis=0)
        high = v.astype(jnp.bfloat16)
        low = (v - high.astype(jnp.float32)).astype(jnp.bfloat16)
        vsplit[0:n, 0:128] = high
        vsplit[0:n, 128:256] = high
        vsplit[n : 2 * n, 0:128] = low
        vsplit[n : 2 * n, 128:256] = low
        for i in range(slots * 128 // WIDE):
            at = pl.ds(i * WIDE, WIDE)
            product = jnp.dot(vsplit[0 : 2 * n], pz[:, at], preferred_element_type=jnp.float32)
            full = plane[0:size, at]
            for k in range(3):
                part = product[k * size : k * size + size] + product[n + k * size : n + k * size + size]
                moved = jnp.sum(part * full, axis=0, keepdims=True)
                for h in range(WIDE // 128):
                    slot = i * (WIDE // 128) + h
                    disp[slot, k : k + 1, :] = (
                        disp[slot, k : k + 1, :] + moved[:, h * 128 : h * 128 + 128]
                    )

    def first(x, packed):
        f = [pop[q, x] for q in range(19)]
        density, momentum = moments(f)
        mom[0, x] = density
        for k in range(3):
            mom[k + 1, x] = momentum[k]
        values = collide(f, density, momentum, None, solid[x] == 1)
        emit(0, x, values)
        return rim(0, x, values, packed)

    def coupled(step):
        def body(x, packed):
            f = [outf[q, x] for q in range(19)]
            values = collide(
                f, mom[0, x], [mom[k, x] for k in range(1, 4)],
                [gfield[k, x] for k in range(3)], solid[x] == 1,
            )
            emit(step, x, values)
            return rim(step, x, values, packed)

        return body

    def driven(x, carry):
        f = [pop[q, x] for q in range(19)]
        values = collide(
            f, mom[0, x], [mom[k, x] for k in range(1, 4)], [gfield[k, x] for k in range(3)],
            solid[x] == 1,
        )
        emit(0, x, values)
        return carry

    def moving(step):
        def body(x, carry):
            stream(step, x)
            return carry

        return body

    for copy in rims:
        copy.wait()
    packed = over_edges(first, jnp.zeros((8, 128), jnp.float32))
    zsend[0, 0] = packed
    x_halos = [halo_x(0)]
    core.wait()
    zsend[0, 1] = over_middle(first, packed)
    yz_halos = [halo_yz(0)]
    for copy in marker_copies:
        copy.wait_recv()
    spread(0, inner, True, mid_terms, mid_plane)
    lax.fori_loop(2, cx - 2, driven, 0, unroll=cx - 4)

    for step in range(STEPS):
        last = step == STEPS - 1
        for copy in yz_halos[step]:
            copy.wait_recv()
        combine(step, False)
        over_middle(moving(step), 0)
        sample(inner if step == 0 else middle, vmid, mid_plane)
        if step == 0:
            spread(1, edges, True, edge_terms, edge_plane)
        for copy in x_halos[step]:
            copy.wait_recv()
        combine(step, True)
        over_edges(moving(step), 0)
        if step > 0:
            sample(edges, vedge, edge_plane)
        if last:
            break
        if step > 0:
            spread(step + 1, edges, True, edge_terms, edge_plane)
        packed = over_edges(coupled(step + 1), jnp.zeros((8, 128), jnp.float32))
        zsend[step + 1, 0] = packed
        x_halos.append(halo_x(step + 1))
        spread(step + 1, middle, False, mid_terms, mid_plane)
        zsend[step + 1, 1] = over_middle(coupled(step + 1), packed)
        yz_halos.append(halo_yz(step + 1))

    for i in range(slots // 2):
        dsend[i] = disp[2 * i] + pltpu.roll(disp[2 * i + 1], 4, axis=0)
    back_copies = exchange(dsend, dback, cap // 2, bsend_sem, brecv_sem)
    for copy in back_copies:
        copy.wait_recv()
    for b in range(blocks):
        tile = jnp.zeros((8, 128), jnp.float32)
        half = jnp.zeros((8, 128), jnp.float32)
        spot = where_to[b]
        for i in range(slots // 2):
            pair = dback[i]
            tile = jnp.where(spot == 2 * i, pair, tile)
            half = jnp.where(spot == 2 * i + 1, pair, half)
        tile = tile + pltpu.roll(half, 4, axis=0)
        for k in range(3):
            outs[k, b : b + 1, :] = tile[k : k + 1, :]
    for copies in [marker_copies] + x_halos + yz_halos + [back_copies]:
        for copy in copies:
            copy.wait_send()


def shards(sizes, populations, solid, marker_pos, anchor_offset, links, patch_col):
    nx, ny, nz, blocks, cap, cx = sizes
    slots = nx * cap
    f32 = jnp.float32
    tile = (8, 128)
    mid = 8 * (cx - 2)
    dma = pltpu.SemaphoreType.DMA
    new, shift = pl.pallas_call(
        functools.partial(kernel, sizes),
        out_shape=(
            pltpu.VMEM(populations.shape, f32),
            pltpu.VMEM((3, blocks, 128), f32),
        ),
        in_specs=[pl.BlockSpec(memory_space=pltpu.HBM)] * 6,
        scratch_shapes=[
            pltpu.VMEM(populations.shape, f32),
            pltpu.VMEM(solid.shape, jnp.int32),
            pltpu.VMEM((3, blocks, 128), f32),
            pltpu.VMEM((3, blocks, 128), f32),
            pltpu.VMEM(links.shape, jnp.int32),
            pltpu.VMEM((1, blocks), jnp.int32),
            pltpu.VMEM((STEPS, 19, cx + 2) + tile, f32),
            pltpu.VMEM((STEPS, 2, 5) + tile, f32),
            pltpu.VMEM((STEPS, 2, 5, 16, 128), f32),
            pltpu.VMEM((STEPS, 2) + tile, f32),
            pltpu.VMEM((STEPS, 5) + tile, f32),
            pltpu.VMEM(tile, f32),
            pltpu.VMEM((4, cx) + tile, f32),
            pltpu.VMEM((3, cx) + tile, f32),
            pltpu.VMEM((3, cx) + tile, f32),
            pltpu.VMEM((96, 256), jnp.bfloat16),
            pltpu.VMEM((6 * mid, 256), jnp.bfloat16),
            pltpu.VMEM((slots,) + tile, f32),
            pltpu.VMEM((slots,) + tile, f32),
            pltpu.VMEM((slots,) + tile, f32),
            pltpu.VMEM((slots,) + tile, f32),
            pltpu.VMEM((slots // 2,) + tile, f32),
            pltpu.VMEM((slots // 2,) + tile, f32),
            pltpu.VMEM((blocks,) + tile, jnp.int32),
            pltpu.VMEM((96, slots * 128), jnp.bfloat16),
            pltpu.VMEM((6 * mid, slots * 128), jnp.bfloat16),
            pltpu.VMEM((256, slots * 128), jnp.bfloat16),
            pltpu.VMEM((16, slots * 128), f32),
            pltpu.VMEM((mid, slots * 128), f32),
            dma((8,)),
            dma((nx,)), dma((nx,)),
            dma((STEPS, 13)), dma((STEPS, 13)),
            dma((nx,)), dma((nx,)),
        ],
        compiler_params=pltpu.CompilerParams(
            collective_id=0, has_side_effects=True, vmem_limit_bytes=62 * 1024 * 1024
        ),
    )(
        populations,
        solid,
        jnp.transpose(marker_pos, (1, 0, 2)),
        jnp.transpose(anchor_offset, (1, 0, 2)),
        links,
        patch_col.T,
    )
    return new, jnp.transpose(shift, (1, 0, 2))


def solution(mesh):
    placed = (
        P(None, "gx", "gy", "gz"),
        P("gx", "gy", "gz"),
        P(("gx", "gy", "gz"), None, None),
        P(("gx", "gy", "gz"), None, None),
        P(("gx", "gy", "gz"), None, None),
        P(("gx", "gy", "gz"), None),
    )

    def whole(populations, solid, marker_pos, anchor_offset, links, patch_col):
        nx, ny, nz = (mesh.shape[name] for name in ("gx", "gy", "gz"))
        blocks = marker_pos.shape[0] // (nx * ny * nz)
        cap = max(2, 2 * blocks // nx)
        sizes = (nx, ny, nz, blocks, cap, populations.shape[1] // nx)
        return jax.shard_map(
            functools.partial(shards, sizes),
            mesh=mesh,
            in_specs=placed,
            out_specs=(P(None, "gx", "gy", "gz"), P(("gx", "gy", "gz"), None, None)),
            check_vma=False,
        )(populations, solid, marker_pos, anchor_offset, links, patch_col)

    return whole
```

```python
import functools

import jax
import jax.numpy as jnp
from jax import lax
from jax.experimental import pallas as pl
from jax.experimental.pallas import tpu as pltpu
from jax.sharding import PartitionSpec as P

STEPS = 3
VELOCITY = (
    (0, 0, 0), (1, 0, 0), (-1, 0, 0), (0, 1, 0), (0, -1, 0), (0, 0, 1), (0, 0, -1),
    (1, 1, 0), (-1, -1, 0), (1, -1, 0), (-1, 1, 0), (1, 0, 1), (-1, 0, -1), (1, 0, -1),
    (-1, 0, 1), (0, 1, 1), (0, -1, -1), (0, 1, -1), (0, -1, 1),
)
WEIGHTS = (1.0 / 3.0,) + (1.0 / 18.0,) * 6 + (1.0 / 36.0,) * 12
OPPOSITE = (0, 2, 1, 4, 3, 6, 5, 8, 7, 10, 9, 12, 11, 14, 13, 16, 15, 18, 17)
TAU = 0.8
K_TETHER = 0.05
K_SPRING = 0.1
NUMBER = {c: q for q, c in enumerate(VELOCITY)}
ORDER = (
    [q for q in range(19) if VELOCITY[q][0] == 0]
    + [q for q in range(19) if VELOCITY[q][0] == 1]
    + [q for q in range(19) if VELOCITY[q][0] == -1]
)
PLACE = {q: i for i, q in enumerate(ORDER)}
Y_MOVERS = [
    [NUMBER[(0, s, 0)], NUMBER[(1, s, 0)], NUMBER[(-1, s, 0)], NUMBER[(0, s, 1)], NUMBER[(0, s, -1)]]
    for s in (1, -1)
]
Z_MOVERS = [
    [NUMBER[(0, 0, s)], NUMBER[(1, 0, s)], NUMBER[(-1, 0, s)], NUMBER[(0, 1, s)], NUMBER[(0, -1, s)]]
    for s in (1, -1)
]
MESH = pl.DeviceIdType.MESH
PARK = -1000.0
SPREAD_UNROLL = 8
CELL_UNROLL = 8
WIDE = 1024
HALF = 64


def axis_sum(values, column):
    total = None
    for q in range(19):
        sign = VELOCITY[q][column]
        if sign == 0:
            continue
        term = values[q]
        total = (term if sign == 1 else -term) if total is None else (
            total + term if sign == 1 else total - term
        )
    return total


def moments(f):
    density = f[0]
    for q in range(1, 19):
        density = density + f[q]
    return density, [axis_sum(f, column) for column in range(3)]


def project(vector, direction):
    total = None
    for column in range(3):
        if direction[column]:
            term = vector[column] if direction[column] == 1 else -vector[column]
            total = term if total is None else total + term
    return total


def collide(f, density, momentum, field, wall):
    over = 1.0 / density
    omega = 1.0 / TAU
    factor = 1.0 - 0.5 / TAU
    if field is None:
        u = [momentum[k] * over for k in range(3)]
    else:
        u = [(momentum[k] + 0.5 * field[k]) * over for k in range(3)]
    square = u[0] * u[0] + u[1] * u[1] + u[2] * u[2]
    base = omega * density * (1.0 - 1.5 * square)
    if field is not None:
        power = u[0] * field[0] + u[1] * field[1] + u[2] * field[2]
        base = base - (3.0 * factor) * power
    scaled = omega * density
    post = [None] * 19
    rest = (1.0 - omega) * f[0] + WEIGHTS[0] * base
    post[0] = jnp.where(wall, f[0], rest)
    for q in range(1, 19, 2):
        p = OPPOSITE[q]
        along = project(u, VELOCITY[q])
        flow = scaled * along
        inner = 4.5 * flow
        odd = 3.0 * flow
        if field is not None:
            pushed = project(field, VELOCITY[q])
            inner = inner + (9.0 * factor) * pushed
            odd = odd + (3.0 * factor) * pushed
        even = WEIGHTS[q] * (base + along * inner)
        odd = WEIGHTS[q] * odd
        post[q] = jnp.where(wall, f[p], (1.0 - omega) * f[q] + (even + odd))
        post[p] = jnp.where(wall, f[q], (1.0 - omega) * f[p] + (even - odd))
    return post


def kernel(
    sizes,
    pop_hbm, solid_hbm, mpos_hbm, moff_hbm, links_hbm, pcol_hbm,
    outf, outs,
    pop, solid, mpos, moff, links, pcol,
    post, ysend, yhalo, zsend, zhalo, zin, mom, gfield, vfield,
    vedge, vmid, pull,
    msend, mrecv, disp, dsend, dback, where_to, edge_terms, mid_terms, pz, edge_plane, mid_plane,
    in_sem, msend_sem, mrecv_sem, hsend_sem, hrecv_sem, bsend_sem, brecv_sem,
):
    nx, ny, nz, blocks, cap, cx = sizes
    slots = nx * cap
    gx, gy, gz = lax.axis_index("gx"), lax.axis_index("gy"), lax.axis_index("gz")
    right, left = lax.rem(gx + 1, nx), lax.rem(gx + nx - 1, nx)
    up, down = lax.rem(gy + 1, ny), lax.rem(gy + ny - 1, ny)
    other = lax.rem(gz + 1, nz)

    def fetch(source, target, n):
        copy = pltpu.make_async_copy(source, target, in_sem.at[n])
        copy.start()
        return copy

    small = [
        fetch(source, target, n)
        for n, (source, target) in enumerate(
            ((pcol_hbm, pcol), (mpos_hbm, mpos), (moff_hbm, moff), (links_hbm, links))
        )
    ]
    barrier = pltpu.get_barrier_semaphore()
    near = [(a, b, gz) for a in (right, left) for b in (up, down)]
    near += [(right, gy, other), (left, gy, other)]
    for o in range(1, nx):
        near.append((lax.rem(gx + o, nx), gy, gz))
    near += [(gx, up, other), (gx, down, other), (gx, up, gz), (gx, down, gz), (gx, gy, other)]
    for device in near:
        pl.semaphore_signal(barrier, inc=1, device_id=device, device_id_type=MESH)
    rims = [
        fetch(pop_hbm.at[:, pl.ds(0, 1)], pop.at[:, pl.ds(0, 1)], 4),
        fetch(pop_hbm.at[:, pl.ds(cx - 1, 1)], pop.at[:, pl.ds(cx - 1, 1)], 5),
        fetch(solid_hbm, solid, 6),
    ]
    core = fetch(pop_hbm.at[:, pl.ds(1, cx - 2)], pop.at[:, pl.ds(1, cx - 2)], 7)

    row = lax.broadcasted_iota(jnp.int32, (8, 128), 0)
    lane = lax.broadcasted_iota(jnp.int32, (8, 128), 1)

    for copy in small:
        copy.wait()
    named = [jnp.broadcast_to(pcol[:, b : b + 1], (8, 128)) for b in range(blocks)]
    spots = []
    for b in range(blocks):
        spot = named[b] * cap
        for e in range(b):
            spot = spot + jnp.where(named[e] == named[b], 1, 0)
        spots.append(spot)
        where_to[b] = spot
    tiles = []
    for b in range(blocks):
        tiles.append(
            jnp.concatenate(
                [mpos[k, b : b + 1, :] for k in range(3)]
                + [moff[k, b : b + 1, :] for k in range(3)]
                + [links[b].astype(jnp.float32)],
                axis=0,
            )
        )
    empty = jnp.where(row < 3, PARK, 0.0)
    for s in range(slots):
        tile = empty
        for b in range(blocks):
            tile = jnp.where(spots[b] == s, tiles[b], tile)
        msend[s] = tile

    pl.semaphore_wait(barrier, len(near))

    peers = []
    low, high = gx * 0, gx * 0 + (nx - 1)
    for _ in range(nx - 1):
        far = jnp.where(high - gx > gx - low, 1, 0)
        peers.append(far * high + (1 - far) * low)
        low, high = low + (1 - far), high - far

    def exchange(source, target, count, send_sem, recv_sem):
        copies = []
        for to in peers:
            o = lax.rem(to + nx - gx, nx)
            copy = pltpu.make_async_remote_copy(
                src_ref=source.at[pl.ds(to * count, count)],
                dst_ref=target.at[pl.ds(gx * count, count)],
                send_sem=send_sem.at[o],
                recv_sem=recv_sem.at[o],
                device_id=(to, gy, gz),
                device_id_type=MESH,
            )
            copy.start()
            copies.append(copy)
        for k in range(count):
            target[gx * count + k] = source[gx * count + k]
        return copies

    marker_copies = exchange(msend, mrecv, cap, msend_sem, mrecv_sem)

    def sender(step, base):
        copies = []

        def go(source, target, device):
            n = base + len(copies)
            copy = pltpu.make_async_remote_copy(
                src_ref=source,
                dst_ref=target,
                send_sem=hsend_sem.at[step, n],
                recv_sem=hrecv_sem.at[step, n],
                device_id=device,
                device_id_type=MESH,
            )
            copy.start()
            copies.append(copy)

        return go, copies

    def halo_x(step):
        go, copies = sender(step, 0)
        for d, b in ((0, up), (1, down)):
            for j, x, a in ((1, cx - 1, right), (2, 0, left)):
                go(
                    ysend.at[step, d, j, pl.ds(x, 1)],
                    yhalo.at[step, d, j, pl.ds(cx, 1)],
                    (a, b, gz),
                )
        z = zsend.at[step, 0]
        go(z, zhalo.at[step, 1], (right, gy, other))
        go(z, zhalo.at[step, 2], (left, gy, other))
        go(post.at[step, pl.ds(9, 5), cx], post.at[step, pl.ds(9, 5), 0], (right, gy, gz))
        go(post.at[step, pl.ds(14, 5), 1], post.at[step, pl.ds(14, 5), cx + 1], (left, gy, gz))
        return copies

    def halo_yz(step):
        go, copies = sender(step, 8)
        z = zsend.at[step, 1]
        go(z, zhalo.at[step, 3], (gx, up, other))
        go(z, zhalo.at[step, 4], (gx, down, other))
        go(ysend.at[step, 0], yhalo.at[step, 0, :, pl.ds(0, cx)], (gx, up, gz))
        go(ysend.at[step, 1], yhalo.at[step, 1, :, pl.ds(0, cx)], (gx, down, gz))
        go(z, zhalo.at[step, 0], (gx, gy, other))
        return copies

    def over_edges(body, carry):
        return lax.fori_loop(0, 2, lambda i, c: body(i * (cx - 1), c), carry, unroll=2)

    def over_middle(body, carry):
        return lax.fori_loop(1, cx - 1, body, carry, unroll=cx - 2)

    def emit(step, x, values):
        for q in range(19):
            post[step, PLACE[q], x + 1] = values[q]

    def rim(step, x, values, packed):
        for d, edge in ((0, 7), (1, 0)):
            for j, q in enumerate(Y_MOVERS[d]):
                ysend[step, d, j, pl.ds(x, 1)] = values[q][edge : edge + 1, :]
        for d, edge in ((0, 127), (1, 0)):
            for j, q in enumerate(Z_MOVERS[d]):
                column = jnp.broadcast_to(values[q][:, edge : edge + 1], (8, 128))
                packed = jnp.where(lane == x + (d * HALF + j * 8), column, packed)
        return packed

    def stream(step, x):
        turned = pltpu.roll(zin[...], lax.rem(128 - x, 128), axis=1)
        f = []
        for q in range(19):
            c = VELOCITY[q]
            tile = post[step, PLACE[q], x + 1 - c[0]]
            if c[1]:
                d = 0 if c[1] == 1 else 1
                j = Y_MOVERS[d].index(q)
                if c[0] == 1:
                    at = lax.rem(x + cx, cx + 1)
                else:
                    at = x - c[0]
                line = jnp.broadcast_to(yhalo[step, d, j, pl.ds(at, 1)], (8, 128))
                tile = jnp.where(row == (0 if d == 0 else 7), line, pltpu.roll(tile, 1 if d == 0 else 7, axis=0))
            if c[2]:
                d = 0 if c[2] == 1 else 1
                j = Z_MOVERS[d].index(q)
                k = d * HALF + j * 8
                column = jnp.broadcast_to(turned[:, k : k + 1], (8, 128))
                tile = jnp.where(
                    lane == (0 if d == 0 else 127), column, pltpu.roll(tile, 1 if d == 0 else 127, axis=1)
                )
            f.append(tile)
            outf[q, x] = tile
        density, momentum = moments(f)
        mom[0, x] = density
        over = 1.0 / density
        for k in range(3):
            mom[k + 1, x] = momentum[k]
            vfield[k, x] = momentum[k] * over

    def combine(step, whole):
        face = zhalo[step, 0]
        group = lax.rem(lane, HALF) // 8
        inside = lax.rem(lane, 8)
        forward = pltpu.roll(face, 1, axis=1)
        backward = pltpu.roll(face, 127, axis=1)
        if whole:
            forward = jnp.where(inside == 0, pltpu.roll(zhalo[step, 1], 121, axis=1), forward)
            backward = jnp.where(inside == 7, pltpu.roll(zhalo[step, 2], 7, axis=1), backward)
        rising = jnp.where(
            row == 0, pltpu.roll(zhalo[step, 3], 1, axis=0), pltpu.roll(face, 1, axis=0)
        )
        falling = jnp.where(
            row == 7, pltpu.roll(zhalo[step, 4], 7, axis=0), pltpu.roll(face, 7, axis=0)
        )
        zin[...] = jnp.where(
            group == 0,
            face,
            jnp.where(
                group == 1,
                forward,
                jnp.where(group == 2, backward, jnp.where(group == 3, rising, falling)),
            ),
        )

    edges = (0, cx - 1)
    middle = tuple(range(1, cx - 1))
    inner = tuple(range(2, cx - 2))

    def spread(step, xs, fresh, terms, plane):
        size = len(xs) * 8
        n = 3 * size
        bf16 = jnp.bfloat16
        depth = lax.broadcasted_iota(jnp.int32, (128, 256), 0).astype(jnp.float32).astype(bf16)
        cell = lax.broadcasted_iota(jnp.int32, (8, 256), 0).astype(jnp.float32)

        def spanned(values, k):
            return jnp.broadcast_to(values[k : k + 1, :], (128, 256)).astype(bf16)

        def one(i, carry):
            pair = [mrecv[2 * i], mrecv[2 * i + 1]]
            info = jnp.concatenate(pair, axis=1)
            if step == 0:
                shift = jnp.zeros((8, 256), jnp.float32)
                disp[i] = shift
            else:
                shift = disp[i]
            position = info + shift
            at = pl.ds(pl.multiple_of(i * 256, 256), 256)
            if fresh:
                force = K_TETHER * ((info + pltpu.roll(info, 5, axis=0)) - position)
                if step > 0:
                    for k in range(2):
                        chosen = jnp.concatenate(
                            [
                                jnp.take_along_axis(
                                    shift[:, h * 128 : h * 128 + 128],
                                    jnp.broadcast_to(pair[h][6 + k : 7 + k, :], (8, 128)).astype(jnp.int32),
                                    axis=1,
                                )
                                for h in range(2)
                            ],
                            axis=1,
                        )
                        force = force + K_SPRING * (chosen - shift)
                    pull[i] = force
                floor = jnp.floor(position)
                above = position - floor
                below = 1.0 - above
                at_floor = depth == spanned(floor, 2)
                at_next = depth == spanned(floor + 1.0, 2)
                for part in range(2):
                    lower = jnp.where(at_next, spanned(above, 2), jnp.zeros((128, 256), bf16))
                    pz[part * 128 : part * 128 + 128, at] = jnp.where(at_floor, spanned(below, 2), lower)
                    below = below - below.astype(bf16).astype(jnp.float32)
                    above = above - above.astype(bf16).astype(jnp.float32)
            else:
                force = pull[i]
            wx = jnp.maximum(0.0, 1.0 - jnp.abs(position[0:1, :] - cell))
            wy = jnp.maximum(0.0, 1.0 - jnp.abs(position[1:2, :] - cell))
            full = jnp.concatenate([wx[x : x + 1, :] * wy for x in xs], axis=0)
            plane[0:size, at] = full
            for k in range(3):
                term = force[k : k + 1, :] * full
                high = term.astype(bf16)
                terms[k * size : k * size + size, at] = high
                terms[n + k * size : n + k * size + size, at] = (term - high.astype(jnp.float32)).astype(bf16)
            return carry

        lax.fori_loop(0, slots // 2, one, 0, unroll=SPREAD_UNROLL)
        total = None
        for h in range(2):
            at = pl.ds(h * slots * 64, slots * 64)
            product = lax.dot_general(
                terms[0 : 2 * n, at], pz[:, at], (((1,), (1,)), ((), ())), preferred_element_type=jnp.float32
            )
            part = product[0:n, 0:128] + (product[0:n, 128:256] + product[n : 2 * n, 0:128])
            total = part if total is None else total + part
        for k in range(3):
            for i, x in enumerate(xs):
                gfield[k, x] = total[k * size + i * 8 : k * size + i * 8 + 8]

    def sample(xs, vsplit, plane):
        size = len(xs) * 8
        n = 3 * size
        v = jnp.concatenate([vfield[k, x] for k in range(3) for x in xs], axis=0)
        high = v.astype(jnp.bfloat16)
        low = (v - high.astype(jnp.float32)).astype(jnp.bfloat16)
        vsplit[0:n, 0:128] = high
        vsplit[0:n, 128:256] = high
        vsplit[n : 2 * n, 0:128] = low
        vsplit[n : 2 * n, 128:256] = low
        for i in range(slots * 128 // WIDE):
            at = pl.ds(i * WIDE, WIDE)
            product = jnp.dot(vsplit[0 : 2 * n], pz[:, at], preferred_element_type=jnp.float32)
            full = plane[0:size, at]
            for k in range(3):
                part = product[k * size : k * size + size] + product[n + k * size : n + k * size + size]
                moved = jnp.sum(part * full, axis=0, keepdims=True)
                for h in range(WIDE // 256):
                    pair = i * (WIDE // 256) + h
                    disp[pair, k : k + 1, :] = (
                        disp[pair, k : k + 1, :] + moved[:, h * 256 : h * 256 + 256]
                    )

    def first(x, packed):
        f = [pop[q, x] for q in range(19)]
        density, momentum = moments(f)
        mom[0, x] = density
        for k in range(3):
            mom[k + 1, x] = momentum[k]
        values = collide(f, density, momentum, None, solid[x] == 1)
        emit(0, x, values)
        return rim(0, x, values, packed)

    def coupled(step):
        def body(x, packed):
            f = [outf[q, x] for q in range(19)]
            values = collide(
                f, mom[0, x], [mom[k, x] for k in range(1, 4)],
                [gfield[k, x] for k in range(3)], solid[x] == 1,
            )
            emit(step, x, values)
            return rim(step, x, values, packed)

        return body

    def driven(x, carry):
        f = [pop[q, x] for q in range(19)]
        values = collide(
            f, mom[0, x], [mom[k, x] for k in range(1, 4)], [gfield[k, x] for k in range(3)],
            solid[x] == 1,
        )
        emit(0, x, values)
        return carry

    def moving(step):
        def body(x, carry):
            stream(step, x)
            return carry

        return body

    for copy in rims:
        copy.wait()
    packed = over_edges(first, jnp.zeros((8, 128), jnp.float32))
    zsend[0, 0] = packed
    x_halos = [halo_x(0)]
    core.wait()
    zsend[0, 1] = over_middle(first, packed)
    yz_halos = [halo_yz(0)]
    for copy in marker_copies:
        copy.wait_recv()
    spread(0, inner, True, mid_terms, mid_plane)
    lax.fori_loop(2, cx - 2, driven, 0, unroll=cx - 4)

    for step in range(STEPS):
        last = step == STEPS - 1
        for copy in yz_halos[step]:
            copy.wait_recv()
        combine(step, False)
        over_middle(moving(step), 0)
        sample(inner if step == 0 else middle, vmid, mid_plane)
        if step == 0:
            spread(1, edges, True, edge_terms, edge_plane)
        for copy in x_halos[step]:
            copy.wait_recv()
        combine(step, True)
        over_edges(moving(step), 0)
        if step > 0:
            sample(edges, vedge, edge_plane)
        if last:
            break
        if step > 0:
            spread(step + 1, edges, True, edge_terms, edge_plane)
        packed = over_edges(coupled(step + 1), jnp.zeros((8, 128), jnp.float32))
        zsend[step + 1, 0] = packed
        x_halos.append(halo_x(step + 1))
        spread(step + 1, middle, False, mid_terms, mid_plane)
        zsend[step + 1, 1] = over_middle(coupled(step + 1), packed)
        yz_halos.append(halo_yz(step + 1))

    for i in range(slots // 2):
        dsend[i] = disp[i, :, 0:128] + pltpu.roll(disp[i, :, 128:256], 4, axis=0)
    back_copies = exchange(dsend, dback, cap // 2, bsend_sem, brecv_sem)
    for copy in back_copies:
        copy.wait_recv()
    for b in range(blocks):
        tile = jnp.zeros((8, 128), jnp.float32)
        half = jnp.zeros((8, 128), jnp.float32)
        spot = where_to[b]
        for i in range(slots // 2):
            pair = dback[i]
            tile = jnp.where(spot == 2 * i, pair, tile)
            half = jnp.where(spot == 2 * i + 1, pair, half)
        tile = tile + pltpu.roll(half, 4, axis=0)
        for k in range(3):
            outs[k, b : b + 1, :] = tile[k : k + 1, :]
    for copies in [marker_copies] + x_halos + yz_halos + [back_copies]:
        for copy in copies:
            copy.wait_send()


def flush(new, shift, new_out, shift_out, a_sem, b_sem):
    a = pltpu.make_async_copy(new, new_out, a_sem)
    b = pltpu.make_async_copy(shift, shift_out, b_sem)
    a.start()
    b.start()
    a.wait()
    b.wait()


def shards(sizes, populations, solid, marker_pos, anchor_offset, links, patch_col):
    nx, ny, nz, blocks, cap, cx = sizes
    slots = nx * cap
    f32 = jnp.float32
    tile = (8, 128)
    mid = 8 * (cx - 2)
    dma = pltpu.SemaphoreType.DMA
    new, shift = pl.pallas_call(
        functools.partial(kernel, sizes),
        out_shape=(
            pltpu.VMEM(populations.shape, f32),
            pltpu.VMEM((3, blocks, 128), f32),
        ),
        in_specs=[pl.BlockSpec(memory_space=pltpu.HBM)] * 6,
        scratch_shapes=[
            pltpu.VMEM(populations.shape, f32),
            pltpu.VMEM(solid.shape, jnp.int32),
            pltpu.VMEM((3, blocks, 128), f32),
            pltpu.VMEM((3, blocks, 128), f32),
            pltpu.VMEM(links.shape, jnp.int32),
            pltpu.VMEM((1, blocks), jnp.int32),
            pltpu.VMEM((STEPS, 19, cx + 2) + tile, f32),
            pltpu.VMEM((STEPS, 2, 5) + tile, f32),
            pltpu.VMEM((STEPS, 2, 5, 16, 128), f32),
            pltpu.VMEM((STEPS, 2) + tile, f32),
            pltpu.VMEM((STEPS, 5) + tile, f32),
            pltpu.VMEM(tile, f32),
            pltpu.VMEM((4, cx) + tile, f32),
            pltpu.VMEM((3, cx) + tile, f32),
            pltpu.VMEM((3, cx) + tile, f32),
            pltpu.VMEM((96, 256), jnp.bfloat16),
            pltpu.VMEM((6 * mid, 256), jnp.bfloat16),
            pltpu.VMEM((slots // 2, 8, 256), f32),
            pltpu.VMEM((slots,) + tile, f32),
            pltpu.VMEM((slots,) + tile, f32),
            pltpu.VMEM((slots // 2, 8, 256), f32),
            pltpu.VMEM((slots // 2,) + tile, f32),
            pltpu.VMEM((slots // 2,) + tile, f32),
            pltpu.VMEM((blocks,) + tile, jnp.int32),
            pltpu.VMEM((96, slots * 128), jnp.bfloat16),
            pltpu.VMEM((6 * mid, slots * 128), jnp.bfloat16),
            pltpu.VMEM((256, slots * 128), jnp.bfloat16),
            pltpu.VMEM((16, slots * 128), f32),
            pltpu.VMEM((mid, slots * 128), f32),
            dma((8,)),
            dma((nx,)), dma((nx,)),
            dma((STEPS, 13)), dma((STEPS, 13)),
            dma((nx,)), dma((nx,)),
        ],
        compiler_params=pltpu.CompilerParams(
            collective_id=0, has_side_effects=True, vmem_limit_bytes=62 * 1024 * 1024
        ),
    )(
        populations,
        solid,
        jnp.transpose(marker_pos, (1, 0, 2)),
        jnp.transpose(anchor_offset, (1, 0, 2)),
        links,
        patch_col.T,
    )
    new, shift = pl.pallas_call(
        flush,
        out_shape=(
            jax.ShapeDtypeStruct(populations.shape, f32),
            jax.ShapeDtypeStruct((3, blocks, 128), f32),
        ),
        in_specs=[pl.BlockSpec(memory_space=pltpu.VMEM)] * 2,
        out_specs=(pl.BlockSpec(memory_space=pltpu.HBM),) * 2,
        scratch_shapes=[dma, dma],
    )(pltpu.with_memory_space_constraint(new, pltpu.VMEM), pltpu.with_memory_space_constraint(shift, pltpu.VMEM))
    return new, jnp.transpose(shift, (1, 0, 2))


def solution(mesh):
    placed = (
        P(None, "gx", "gy", "gz"),
        P("gx", "gy", "gz"),
        P(("gx", "gy", "gz"), None, None),
        P(("gx", "gy", "gz"), None, None),
        P(("gx", "gy", "gz"), None, None),
        P(("gx", "gy", "gz"), None),
    )

    def whole(populations, solid, marker_pos, anchor_offset, links, patch_col):
        nx, ny, nz = (mesh.shape[name] for name in ("gx", "gy", "gz"))
        blocks = marker_pos.shape[0] // (nx * ny * nz)
        cap = max(2, 2 * blocks // nx)
        sizes = (nx, ny, nz, blocks, cap, populations.shape[1] // nx)
        return jax.shard_map(
            functools.partial(shards, sizes),
            mesh=mesh,
            in_specs=placed,
            out_specs=(P(None, "gx", "gy", "gz"), P(("gx", "gy", "gz"), None, None)),
            check_vma=False,
        )(populations, solid, marker_pos, anchor_offset, links, patch_col)

    return whole
```

```python
import functools

import jax
import jax.numpy as jnp
from jax import lax
from jax.experimental import pallas as pl
from jax.experimental.pallas import tpu as pltpu
from jax.sharding import PartitionSpec as P

STEPS = 3
VELOCITY = (
    (0, 0, 0), (1, 0, 0), (-1, 0, 0), (0, 1, 0), (0, -1, 0), (0, 0, 1), (0, 0, -1),
    (1, 1, 0), (-1, -1, 0), (1, -1, 0), (-1, 1, 0), (1, 0, 1), (-1, 0, -1), (1, 0, -1),
    (-1, 0, 1), (0, 1, 1), (0, -1, -1), (0, 1, -1), (0, -1, 1),
)
WEIGHTS = (1.0 / 3.0,) + (1.0 / 18.0,) * 6 + (1.0 / 36.0,) * 12
OPPOSITE = (0, 2, 1, 4, 3, 6, 5, 8, 7, 10, 9, 12, 11, 14, 13, 16, 15, 18, 17)
TAU = 0.8
K_TETHER = 0.05
K_SPRING = 0.1
NUMBER = {c: q for q, c in enumerate(VELOCITY)}
ORDER = (
    [q for q in range(19) if VELOCITY[q][0] == 0]
    + [q for q in range(19) if VELOCITY[q][0] == 1]
    + [q for q in range(19) if VELOCITY[q][0] == -1]
)
PLACE = {q: i for i, q in enumerate(ORDER)}
Y_MOVERS = [
    [NUMBER[(0, s, 0)], NUMBER[(1, s, 0)], NUMBER[(-1, s, 0)], NUMBER[(0, s, 1)], NUMBER[(0, s, -1)]]
    for s in (1, -1)
]
Z_MOVERS = [
    [NUMBER[(0, 0, s)], NUMBER[(1, 0, s)], NUMBER[(-1, 0, s)], NUMBER[(0, 1, s)], NUMBER[(0, -1, s)]]
    for s in (1, -1)
]
MESH = pl.DeviceIdType.MESH
PARK = -1000.0
CELL_UNROLL = 8
WIDE = 1024
HALF = 64


def axis_sum(values, column):
    total = None
    for q in range(19):
        sign = VELOCITY[q][column]
        if sign == 0:
            continue
        term = values[q]
        total = (term if sign == 1 else -term) if total is None else (
            total + term if sign == 1 else total - term
        )
    return total


def moments(f):
    density = f[0]
    for q in range(1, 19):
        density = density + f[q]
    return density, [axis_sum(f, column) for column in range(3)]


def project(vector, direction):
    total = None
    for column in range(3):
        if direction[column]:
            term = vector[column] if direction[column] == 1 else -vector[column]
            total = term if total is None else total + term
    return total


def collide(f, density, momentum, field, wall):
    over = 1.0 / density
    omega = 1.0 / TAU
    factor = 1.0 - 0.5 / TAU
    if field is None:
        u = [momentum[k] * over for k in range(3)]
    else:
        u = [(momentum[k] + 0.5 * field[k]) * over for k in range(3)]
    square = u[0] * u[0] + u[1] * u[1] + u[2] * u[2]
    base = omega * density * (1.0 - 1.5 * square)
    if field is not None:
        power = u[0] * field[0] + u[1] * field[1] + u[2] * field[2]
        base = base - (3.0 * factor) * power
    post = [None] * 19
    rest = (1.0 - omega) * f[0] + WEIGHTS[0] * base
    post[0] = jnp.where(wall, f[0], rest)
    for numbers in (range(1, 7, 2), range(7, 19, 2)):
        weight = WEIGHTS[numbers[0]]
        level = weight * base
        scaled = (4.5 * weight * omega) * density
        if field is not None:
            push = [(4.5 * factor * weight) * field[k] for k in range(3)]
        for q in numbers:
            p = OPPOSITE[q]
            along = project(u, VELOCITY[q])
            flow = scaled * along
            if field is None:
                odd = (2.0 / 3.0) * flow
                even = level + along * flow
            else:
                pushed = project(push, VELOCITY[q])
                flow = flow + pushed
                odd = (2.0 / 3.0) * flow
                even = level + along * (flow + pushed)
            post[q] = jnp.where(wall, f[p], (1.0 - omega) * f[q] + (even + odd))
            post[p] = jnp.where(wall, f[q], (1.0 - omega) * f[p] + (even - odd))
    return post


def kernel(
    sizes,
    pop_hbm, solid_hbm, mpos_hbm, moff_hbm, links_hbm, pcol_hbm,
    outf, outs,
    pop, solid, mpos, moff, links, pcol,
    post, ysend, yhalo, zsend, zhalo, zin, mom, gfield, vfield,
    vedge, vmid, pull,
    msend, mrecv, lsend, lrecv, disp, dsend, dback, where_to,
    edge_terms, mid_terms, pz, edge_plane, mid_plane,
    csend_sem, mrecv_sem, lrecv_sem, brecv_sem, hsend_sem, hrecv_sem,
):
    nx, ny, nz, blocks, cap, cx = sizes
    slots = nx * cap
    gx, gy, gz = lax.axis_index("gx"), lax.axis_index("gy"), lax.axis_index("gz")
    right, left = lax.rem(gx + 1, nx), lax.rem(gx + nx - 1, nx)
    up, down = lax.rem(gy + 1, ny), lax.rem(gy + ny - 1, ny)
    other = lax.rem(gz + 1, nz)

    def fetch(source, target, n):
        copy = pltpu.make_async_copy(source, target, hsend_sem.at[n])
        copy.start()
        return copy

    small = [
        fetch(source, target, n)
        for n, (source, target) in enumerate(
            ((pcol_hbm, pcol), (mpos_hbm, mpos), (moff_hbm, moff), (links_hbm, links))
        )
    ]
    barrier = pltpu.get_barrier_semaphore()
    near = [(a, b, gz) for a in (right, left) for b in (up, down)]
    near += [(right, gy, other), (left, gy, other)]
    for o in range(1, nx):
        near.append((lax.rem(gx + o, nx), gy, gz))
    near += [(gx, up, other), (gx, down, other), (gx, up, gz), (gx, down, gz), (gx, gy, other)]
    for device in near:
        pl.semaphore_signal(barrier, inc=1, device_id=device, device_id_type=MESH)
    rims = [
        fetch(pop_hbm.at[:, pl.ds(0, 1)], pop.at[:, pl.ds(0, 1)], 4),
        fetch(pop_hbm.at[:, pl.ds(cx - 1, 1)], pop.at[:, pl.ds(cx - 1, 1)], 5),
        fetch(solid_hbm, solid, 6),
    ]
    core = fetch(pop_hbm.at[:, pl.ds(1, cx - 2)], pop.at[:, pl.ds(1, cx - 2)], 8)

    row = lax.broadcasted_iota(jnp.int32, (8, 128), 0)
    lane = lax.broadcasted_iota(jnp.int32, (8, 128), 1)

    for copy in small:
        copy.wait()
    named = [jnp.broadcast_to(pcol[:, b : b + 1], (8, 128)) for b in range(blocks)]
    spots = []
    for b in range(blocks):
        spot = named[b] * cap
        for e in range(b):
            spot = spot + jnp.where(named[e] == named[b], 1, 0)
        spots.append(spot)
        where_to[b] = spot
    tiles = []
    for b in range(blocks):
        tiles.append(
            jnp.concatenate(
                [mpos[k, b : b + 1, :] for k in range(3)]
                + [moff[k, b : b + 1, :] for k in range(3)]
                + [links[b].astype(jnp.float32)],
                axis=0,
            )
        )
    empty = jnp.where(row < 3, PARK, 0.0)
    for s in range(slots):
        tile = empty
        for b in range(blocks):
            tile = jnp.where(spots[b] == s, tiles[b], tile)
        g, c = s // cap, s % cap
        msend[g, 6 * c : 6 * c + 6, :] = tile[0:6, :]
        lsend[g, 2 * c : 2 * c + 2, :] = tile[6:8, :]

    pl.semaphore_wait(barrier, len(near))

    peers = []
    low, high = gx * 0, gx * 0 + (nx - 1)
    for _ in range(nx - 1):
        far = jnp.where(high - gx > gx - low, 1, 0)
        peers.append(far * high + (1 - far) * low)
        low, high = low + (1 - far), high - far

    origins = [gx] + peers[::-1]

    def exchange(source, target, rows, send_sem, recv_sem):
        copies = []
        for to in peers:
            copy = pltpu.make_async_remote_copy(
                src_ref=source.at[to, pl.ds(0, rows)],
                dst_ref=target.at[gx, pl.ds(0, rows)],
                send_sem=send_sem.at[to],
                recv_sem=recv_sem.at[gx],
                device_id=(to, gy, gz),
                device_id_type=MESH,
            )
            copy.start()
            copies.append(copy)
        target[gx, 0:rows, :] = source[gx, 0:rows, :]
        return copies

    def arrive(source, target, rows, send_sem, recv_sem, origin):
        pltpu.make_async_remote_copy(
            src_ref=source.at[origin, pl.ds(0, rows)],
            dst_ref=target.at[origin, pl.ds(0, rows)],
            send_sem=send_sem.at[origin],
            recv_sem=recv_sem.at[origin],
            device_id=(origin, gy, gz),
            device_id_type=MESH,
        ).wait_recv()

    places = (msend, mrecv, 6 * cap, csend_sem.at[0], mrecv_sem)
    tethers = (lsend, lrecv, 2 * cap, csend_sem.at[1], lrecv_sem)
    returns = (dsend, dback, 3 * cap, csend_sem.at[0], brecv_sem)
    place_copies = exchange(*places)
    for g in range(nx):
        mrecv[g, 6 * cap : 6 * cap + 2, :] = jnp.zeros((2, 128), jnp.float32)

    def sender(step, base):
        copies = []

        def go(source, target, device):
            n = base + len(copies)
            copy = pltpu.make_async_remote_copy(
                src_ref=source,
                dst_ref=target,
                send_sem=hsend_sem.at[n],
                recv_sem=hrecv_sem.at[step % 2, n],
                device_id=device,
                device_id_type=MESH,
            )
            copy.start()
            copies.append(copy)

        return go, copies

    def halo_x(step):
        go, copies = sender(step, 0)
        for d, b in ((0, up), (1, down)):
            for j, x, a in ((1, cx - 1, right), (2, 0, left)):
                go(
                    ysend.at[step, d, j, pl.ds(x, 1)],
                    yhalo.at[step, d, j, pl.ds(cx, 1)],
                    (a, b, gz),
                )
        z = zsend.at[step, 0]
        go(z, zhalo.at[step, 1], (right, gy, other))
        go(z, zhalo.at[step, 2], (left, gy, other))
        go(post.at[step, pl.ds(9, 5), cx], post.at[step, pl.ds(9, 5), 0], (right, gy, gz))
        go(post.at[step, pl.ds(14, 5), 1], post.at[step, pl.ds(14, 5), cx + 1], (left, gy, gz))
        return copies

    def halo_yz(step):
        go, copies = sender(step, 8)
        z = zsend.at[step, 1]
        go(z, zhalo.at[step, 3], (gx, up, other))
        go(z, zhalo.at[step, 4], (gx, down, other))
        go(ysend.at[step, 0], yhalo.at[step, 0, :, pl.ds(0, cx)], (gx, up, gz))
        go(ysend.at[step, 1], yhalo.at[step, 1, :, pl.ds(0, cx)], (gx, down, gz))
        go(z, zhalo.at[step, 0], (gx, gy, other))
        return copies

    def over_edges(body, carry):
        return lax.fori_loop(0, 2, lambda i, c: body(i * (cx - 1), c), carry, unroll=2)

    def over_middle(body, carry):
        return lax.fori_loop(1, cx - 1, body, carry, unroll=cx - 2)

    def emit(step, x, values):
        for q in range(19):
            post[step, PLACE[q], x + 1] = values[q]

    def rim(step, x, values, packed):
        for d, edge in ((0, 7), (1, 0)):
            for j, q in enumerate(Y_MOVERS[d]):
                ysend[step, d, j, pl.ds(x, 1)] = values[q][edge : edge + 1, :]
        for d, edge in ((0, 127), (1, 0)):
            for j, q in enumerate(Z_MOVERS[d]):
                column = jnp.broadcast_to(values[q][:, edge : edge + 1], (8, 128))
                packed = jnp.where(lane == x + (d * HALF + j * 8), column, packed)
        return packed

    def stream(step, x):
        turned = pltpu.roll(zin[...], lax.rem(128 - x, 128), axis=1)
        f = []
        for q in range(19):
            c = VELOCITY[q]
            tile = post[step, PLACE[q], x + 1 - c[0]]
            if c[1]:
                d = 0 if c[1] == 1 else 1
                j = Y_MOVERS[d].index(q)
                if c[0] == 1:
                    at = lax.rem(x + cx, cx + 1)
                else:
                    at = x - c[0]
                line = jnp.broadcast_to(yhalo[step, d, j, pl.ds(at, 1)], (8, 128))
                tile = jnp.where(row == (0 if d == 0 else 7), line, pltpu.roll(tile, 1 if d == 0 else 7, axis=0))
            if c[2]:
                d = 0 if c[2] == 1 else 1
                j = Z_MOVERS[d].index(q)
                k = d * HALF + j * 8
                column = jnp.broadcast_to(turned[:, k : k + 1], (8, 128))
                tile = jnp.where(
                    lane == (0 if d == 0 else 127), column, pltpu.roll(tile, 1 if d == 0 else 127, axis=1)
                )
            f.append(tile)
            outf[q, x] = tile
        density, momentum = moments(f)
        mom[0, x] = density
        over = 1.0 / density
        for k in range(3):
            mom[k + 1, x] = momentum[k]
            vfield[k, x] = momentum[k] * over

    def combine(step, whole):
        face = zhalo[step, 0]
        group = lax.rem(lane, HALF) // 8
        inside = lax.rem(lane, 8)
        forward = pltpu.roll(face, 1, axis=1)
        backward = pltpu.roll(face, 127, axis=1)
        if whole:
            forward = jnp.where(inside == 0, pltpu.roll(zhalo[step, 1], 121, axis=1), forward)
            backward = jnp.where(inside == 7, pltpu.roll(zhalo[step, 2], 7, axis=1), backward)
        rising = jnp.where(
            row == 0, pltpu.roll(zhalo[step, 3], 1, axis=0), pltpu.roll(face, 1, axis=0)
        )
        falling = jnp.where(
            row == 7, pltpu.roll(zhalo[step, 4], 7, axis=0), pltpu.roll(face, 7, axis=0)
        )
        zin[...] = jnp.where(
            group == 0,
            face,
            jnp.where(
                group == 1,
                forward,
                jnp.where(group == 2, backward, jnp.where(group == 3, rising, falling)),
            ),
        )

    edges = (0, cx - 1)
    middle = tuple(range(1, cx - 1))
    inner = tuple(range(2, cx - 2))

    def spread(step, xs, fresh, terms, plane):
        size = len(xs) * 8
        n = 3 * size
        f32, bf16 = jnp.float32, jnp.bfloat16
        depth = lax.broadcasted_iota(jnp.int32, (128, 256), 0).astype(f32).astype(bf16)
        cell = lax.broadcasted_iota(jnp.int32, (8, 256), 0).astype(f32)

        def spanned(values, k):
            return jnp.broadcast_to(values[k : k + 1, :], (128, 256)).astype(bf16)

        def one(turn, h):
            g = origins[turn]
            i = turn * (cap // 2) + h
            info = jnp.concatenate([mrecv[g, pl.ds(6 * (2 * h + e), 8), :] for e in range(2)], axis=1)
            if step == 0:
                position = info
                disp[i] = jnp.zeros((8, 256), f32)
            else:
                shift = disp[i]
                position = info + shift
            at = pl.ds(i * 256, 256)
            if fresh:
                force = K_TETHER * ((info + pltpu.roll(info, 5, axis=0)) - position)
                if step > 0:
                    for k in range(2):
                        chosen = jnp.concatenate(
                            [
                                jnp.take_along_axis(
                                    shift[:, e * 128 : e * 128 + 128],
                                    jnp.broadcast_to(lrecv[g, pl.ds(2 * (2 * h + e) + k, 1), :], (8, 128)).astype(jnp.int32),
                                    axis=1,
                                )
                                for e in range(2)
                            ],
                            axis=1,
                        )
                        force = force + K_SPRING * (chosen - shift)
                    pull[i] = force
                floor = jnp.floor(position)
                above = position - floor
                below = 1.0 - above
                at_floor = depth == spanned(floor, 2)
                at_next = depth == spanned(floor + 1.0, 2)
                for part in range(2):
                    lower = jnp.where(at_next, spanned(above, 2), jnp.zeros((128, 256), bf16))
                    pz[part * 128 : part * 128 + 128, at] = jnp.where(at_floor, spanned(below, 2), lower)
                    below = below - below.astype(bf16).astype(f32)
                    above = above - above.astype(bf16).astype(f32)
            else:
                force = pull[i]
            wx = jnp.maximum(0.0, 1.0 - jnp.abs(position[0:1, :] - cell))
            wy = jnp.maximum(0.0, 1.0 - jnp.abs(position[1:2, :] - cell))
            full = jnp.concatenate([wx[x : x + 1, :] * wy for x in xs], axis=0)
            plane[0:size, at] = full
            for k in range(3):
                term = force[k : k + 1, :] * full
                high = term.astype(bf16)
                terms[k * size : k * size + size, at] = high
                terms[n + k * size : n + k * size + size, at] = (term - high.astype(f32)).astype(bf16)

        def gather(at):
            product = lax.dot_general(
                terms[0 : 2 * n, at], pz[:, at], (((1,), (1,)), ((), ())), preferred_element_type=f32
            )
            return product[0:n, 0:128] + (product[0:n, 128:256] + product[n : 2 * n, 0:128])

        total = None
        for turn in range(nx):
            if step == 0 and turn:
                arrive(*places, origins[turn])
            for h in range(cap // 2):
                one(turn, h)
            if step == 0:
                part = gather(pl.ds(turn * (cap * 128), cap * 128))
                total = part if total is None else total + part
        if step > 0:
            for h in range(2):
                part = gather(pl.ds(h * slots * 64, slots * 64))
                total = part if total is None else total + part
        for k in range(3):
            for i, x in enumerate(xs):
                gfield[k, x] = total[k * size + i * 8 : k * size + i * 8 + 8]

    def sample(xs, vsplit, plane):
        size = len(xs) * 8
        n = 3 * size
        v = jnp.concatenate([vfield[k, x] for k in range(3) for x in xs], axis=0)
        high = v.astype(jnp.bfloat16)
        low = (v - high.astype(jnp.float32)).astype(jnp.bfloat16)
        vsplit[0:n, 0:128] = high
        vsplit[0:n, 128:256] = high
        vsplit[n : 2 * n, 0:128] = low
        vsplit[n : 2 * n, 128:256] = low
        for i in range(slots * 128 // WIDE):
            at = pl.ds(i * WIDE, WIDE)
            product = jnp.dot(vsplit[0 : 2 * n], pz[:, at], preferred_element_type=jnp.float32)
            full = plane[0:size, at]
            for k in range(3):
                part = product[k * size : k * size + size] + product[n + k * size : n + k * size + size]
                moved = jnp.sum(part * full, axis=0, keepdims=True)
                for h in range(WIDE // 256):
                    pair = i * (WIDE // 256) + h
                    disp[pair, k : k + 1, :] = (
                        disp[pair, k : k + 1, :] + moved[:, h * 256 : h * 256 + 256]
                    )

    def first(x, packed):
        f = [pop[q, x] for q in range(19)]
        density, momentum = moments(f)
        mom[0, x] = density
        for k in range(3):
            mom[k + 1, x] = momentum[k]
        values = collide(f, density, momentum, None, solid[x] == 1)
        emit(0, x, values)
        return rim(0, x, values, packed)

    def coupled(step):
        def body(x, packed):
            f = [outf[q, x] for q in range(19)]
            values = collide(
                f, mom[0, x], [mom[k, x] for k in range(1, 4)],
                [gfield[k, x] for k in range(3)], solid[x] == 1,
            )
            emit(step, x, values)
            return rim(step, x, values, packed)

        return body

    def driven(x, carry):
        f = [pop[q, x] for q in range(19)]
        values = collide(
            f, mom[0, x], [mom[k, x] for k in range(1, 4)], [gfield[k, x] for k in range(3)],
            solid[x] == 1,
        )
        emit(0, x, values)
        return carry

    def moving(step):
        def body(x, carry):
            stream(step, x)
            return carry

        return body

    for copy in rims:
        copy.wait()
    packed = over_edges(first, jnp.zeros((8, 128), jnp.float32))
    zsend[0, 0] = packed
    x_halos = [halo_x(0)]
    core.wait()
    zsend[0, 1] = over_middle(first, packed)
    yz_halos = [halo_yz(0)]
    link_copies = exchange(*tethers)
    spread(0, inner, True, mid_terms, mid_plane)
    lax.fori_loop(2, cx - 2, driven, 0, unroll=cx - 4)

    for step in range(STEPS):
        last = step == STEPS - 1
        for copy in yz_halos[step]:
            copy.wait_recv()
        combine(step, False)
        over_middle(moving(step), 0)
        sample(inner if step == 0 else middle, vmid, mid_plane)
        if step == 0:
            for g in peers[::-1]:
                arrive(*tethers, g)
            spread(1, edges, True, edge_terms, edge_plane)
        for copy in x_halos[step]:
            copy.wait_recv()
        combine(step, True)
        over_edges(moving(step), 0)
        if step > 0:
            sample(edges, vedge, edge_plane)
        if last:
            break
        if step > 0:
            spread(step + 1, edges, True, edge_terms, edge_plane)
        packed = over_edges(coupled(step + 1), jnp.zeros((8, 128), jnp.float32))
        zsend[step + 1, 0] = packed
        for copy in x_halos[step]:
            copy.wait_send()
        x_halos.append(halo_x(step + 1))
        spread(step + 1, middle, False, mid_terms, mid_plane)
        zsend[step + 1, 1] = over_middle(coupled(step + 1), packed)
        for copy in yz_halos[step]:
            copy.wait_send()
        yz_halos.append(halo_yz(step + 1))

    for copy in place_copies:
        copy.wait_send()
    for c in range(slots):
        h = (c % 2) * 128
        at = 3 * (c % cap)
        dsend[origins[c // cap], at : at + 3, :] = disp[c // 2, 0:3, h : h + 128]
    back_copies = exchange(*returns)
    for copies in [link_copies, x_halos[-1], yz_halos[-1]]:
        for copy in copies:
            copy.wait_send()
    for g in peers[::-1]:
        arrive(*returns, g)
    tiles = [jnp.zeros((3, 128), jnp.float32) for b in range(blocks)]
    for c in range(slots):
        at = 3 * (c % cap)
        came = dback[c // cap, at : at + 3, :]
        tiles = [jnp.where(where_to[b, 0:3, :] == c, came, tiles[b]) for b in range(blocks)]
    for b in range(blocks):
        for k in range(3):
            outs[k, b : b + 1, :] = tiles[b][k : k + 1, :]
    for copy in back_copies:
        copy.wait_send()


def flush(new, shift, new_out, shift_out, a_sem, b_sem):
    a = pltpu.make_async_copy(new, new_out, a_sem)
    b = pltpu.make_async_copy(shift, shift_out, b_sem)
    a.start()
    b.start()
    a.wait()
    b.wait()


def shards(sizes, populations, solid, marker_pos, anchor_offset, links, patch_col):
    nx, ny, nz, blocks, cap, cx = sizes
    slots = nx * cap
    f32 = jnp.float32
    tile = (8, 128)
    mid = 8 * (cx - 2)
    padded = lambda rows: -(-rows // 8) * 8
    dma = pltpu.SemaphoreType.DMA
    new, shift = pl.pallas_call(
        functools.partial(kernel, sizes),
        out_shape=(
            pltpu.VMEM(populations.shape, f32),
            pltpu.VMEM((3, blocks, 128), f32),
        ),
        in_specs=[pl.BlockSpec(memory_space=pltpu.HBM)] * 6,
        scratch_shapes=[
            pltpu.VMEM(populations.shape, f32),
            pltpu.VMEM(solid.shape, jnp.int32),
            pltpu.VMEM((3, blocks, 128), f32),
            pltpu.VMEM((3, blocks, 128), f32),
            pltpu.VMEM(links.shape, jnp.int32),
            pltpu.VMEM((1, blocks), jnp.int32),
            pltpu.VMEM((STEPS, 19, cx + 2) + tile, f32),
            pltpu.VMEM((STEPS, 2, 5) + tile, f32),
            pltpu.VMEM((STEPS, 2, 5, 16, 128), f32),
            pltpu.VMEM((STEPS, 2) + tile, f32),
            pltpu.VMEM((STEPS, 5) + tile, f32),
            pltpu.VMEM(tile, f32),
            pltpu.VMEM((4, cx) + tile, f32),
            pltpu.VMEM((3, cx) + tile, f32),
            pltpu.VMEM((3, cx) + tile, f32),
            pltpu.VMEM((96, 256), jnp.bfloat16),
            pltpu.VMEM((6 * mid, 256), jnp.bfloat16),
            pltpu.VMEM((slots // 2, 8, 256), f32),
            pltpu.VMEM((nx, padded(6 * cap), 128), f32),
            pltpu.VMEM((nx, padded(6 * cap + 2), 128), f32),
            pltpu.VMEM((nx, padded(2 * cap), 128), f32),
            pltpu.VMEM((nx, padded(2 * cap), 128), f32),
            pltpu.VMEM((slots // 2, 8, 256), f32),
            pltpu.VMEM((nx, padded(3 * cap), 128), f32),
            pltpu.VMEM((nx, padded(3 * cap), 128), f32),
            pltpu.VMEM((blocks,) + tile, jnp.int32),
            pltpu.VMEM((96, slots * 128), jnp.bfloat16),
            pltpu.VMEM((6 * mid, slots * 128), jnp.bfloat16),
            pltpu.VMEM((256, slots * 128), jnp.bfloat16),
            pltpu.VMEM((16, slots * 128), f32),
            pltpu.VMEM((mid, slots * 128), f32),
            dma((2, nx)), dma((nx,)), dma((nx,)), dma((nx,)),
            dma((13,)), dma((2, 13)),
        ],
        compiler_params=pltpu.CompilerParams(
            collective_id=0, has_side_effects=True, vmem_limit_bytes=62 * 1024 * 1024
        ),
    )(
        populations,
        solid,
        jnp.transpose(marker_pos, (1, 0, 2)),
        jnp.transpose(anchor_offset, (1, 0, 2)),
        links,
        patch_col.T,
    )
    new, shift = pl.pallas_call(
        flush,
        out_shape=(
            jax.ShapeDtypeStruct(populations.shape, f32),
            jax.ShapeDtypeStruct((3, blocks, 128), f32),
        ),
        in_specs=[pl.BlockSpec(memory_space=pltpu.VMEM)] * 2,
        out_specs=(pl.BlockSpec(memory_space=pltpu.HBM),) * 2,
        scratch_shapes=[dma, dma],
    )(pltpu.with_memory_space_constraint(new, pltpu.VMEM), pltpu.with_memory_space_constraint(shift, pltpu.VMEM))
    return new, jnp.transpose(shift, (1, 0, 2))


def solution(mesh):
    placed = (
        P(None, "gx", "gy", "gz"),
        P("gx", "gy", "gz"),
        P(("gx", "gy", "gz"), None, None),
        P(("gx", "gy", "gz"), None, None),
        P(("gx", "gy", "gz"), None, None),
        P(("gx", "gy", "gz"), None),
    )

    def whole(populations, solid, marker_pos, anchor_offset, links, patch_col):
        nx, ny, nz = (mesh.shape[name] for name in ("gx", "gy", "gz"))
        blocks = marker_pos.shape[0] // (nx * ny * nz)
        cap = max(2, 2 * blocks // nx)
        sizes = (nx, ny, nz, blocks, cap, populations.shape[1] // nx)
        return jax.shard_map(
            functools.partial(shards, sizes),
            mesh=mesh,
            in_specs=placed,
            out_specs=(P(None, "gx", "gy", "gz"), P(("gx", "gy", "gz"), None, None)),
            check_vma=False,
        )(populations, solid, marker_pos, anchor_offset, links, patch_col)

    return whole
```

```python
import functools

import jax
import jax.numpy as jnp
from jax import lax
from jax.experimental import pallas as pl
from jax.experimental.pallas import tpu as pltpu
from jax.sharding import PartitionSpec as P

STEPS = 3
VELOCITY = (
    (0, 0, 0), (1, 0, 0), (-1, 0, 0), (0, 1, 0), (0, -1, 0), (0, 0, 1), (0, 0, -1),
    (1, 1, 0), (-1, -1, 0), (1, -1, 0), (-1, 1, 0), (1, 0, 1), (-1, 0, -1), (1, 0, -1),
    (-1, 0, 1), (0, 1, 1), (0, -1, -1), (0, 1, -1), (0, -1, 1),
)
WEIGHTS = (1.0 / 3.0,) + (1.0 / 18.0,) * 6 + (1.0 / 36.0,) * 12
OPPOSITE = (0, 2, 1, 4, 3, 6, 5, 8, 7, 10, 9, 12, 11, 14, 13, 16, 15, 18, 17)
TAU = 0.8
K_TETHER = 0.05
K_SPRING = 0.1
NUMBER = {c: q for q, c in enumerate(VELOCITY)}
ORDER = (
    [q for q in range(19) if VELOCITY[q][0] == 0]
    + [q for q in range(19) if VELOCITY[q][0] == 1]
    + [q for q in range(19) if VELOCITY[q][0] == -1]
)
PLACE = {q: i for i, q in enumerate(ORDER)}
Y_MOVERS = [
    [NUMBER[(0, s, 0)], NUMBER[(1, s, 0)], NUMBER[(-1, s, 0)], NUMBER[(0, s, 1)], NUMBER[(0, s, -1)]]
    for s in (1, -1)
]
Z_MOVERS = [
    [NUMBER[(0, 0, s)], NUMBER[(1, 0, s)], NUMBER[(-1, 0, s)], NUMBER[(0, 1, s)], NUMBER[(0, -1, s)]]
    for s in (1, -1)
]
MESH = pl.DeviceIdType.MESH
PARK = -1000.0
CELL_UNROLL = 8
WIDE = 1024
HALF = 64


def axis_sum(values, column):
    total = None
    for q in range(19):
        sign = VELOCITY[q][column]
        if sign == 0:
            continue
        term = values[q]
        total = (term if sign == 1 else -term) if total is None else (
            total + term if sign == 1 else total - term
        )
    return total


def moments(f):
    density = f[0]
    for q in range(1, 19):
        density = density + f[q]
    return density, [axis_sum(f, column) for column in range(3)]


def project(vector, direction):
    total = None
    for column in range(3):
        if direction[column]:
            term = vector[column] if direction[column] == 1 else -vector[column]
            total = term if total is None else total + term
    return total


def collide(f, density, momentum, field, wall):
    over = 1.0 / density
    omega = 1.0 / TAU
    factor = 1.0 - 0.5 / TAU
    if field is None:
        u = [momentum[k] * over for k in range(3)]
    else:
        u = [(momentum[k] + 0.5 * field[k]) * over for k in range(3)]
    square = u[0] * u[0] + u[1] * u[1] + u[2] * u[2]
    base = omega * density * (1.0 - 1.5 * square)
    if field is not None:
        power = u[0] * field[0] + u[1] * field[1] + u[2] * field[2]
        base = base - (3.0 * factor) * power
    post = [None] * 19
    rest = (1.0 - omega) * f[0] + WEIGHTS[0] * base
    post[0] = jnp.where(wall, f[0], rest)
    for numbers in (range(1, 7, 2), range(7, 19, 2)):
        weight = WEIGHTS[numbers[0]]
        level = weight * base
        scaled = (4.5 * weight * omega) * density
        if field is not None:
            push = [(4.5 * factor * weight) * field[k] for k in range(3)]
        for q in numbers:
            p = OPPOSITE[q]
            along = project(u, VELOCITY[q])
            flow = scaled * along
            if field is None:
                odd = (2.0 / 3.0) * flow
                even = level + along * flow
            else:
                pushed = project(push, VELOCITY[q])
                flow = flow + pushed
                odd = (2.0 / 3.0) * flow
                even = level + along * (flow + pushed)
            post[q] = jnp.where(wall, f[p], (1.0 - omega) * f[q] + (even + odd))
            post[p] = jnp.where(wall, f[q], (1.0 - omega) * f[p] + (even - odd))
    return post


def kernel(
    sizes,
    pop_hbm, solid_hbm, mpos_hbm, moff_hbm, links_hbm, pcol_hbm,
    outf, outs,
    pop, solid, mpos, moff, links, pcol,
    post, ysend, yhalo, zsend, zhalo, zin, mom, gfield, vfield,
    vedge, vmid, pull,
    msend, mrecv, lsend, lrecv, disp, dsend, dback, where_to,
    edge_terms, mid_terms, pz, edge_plane, mid_plane,
    csend_sem, mrecv_sem, lrecv_sem, brecv_sem, hsend_sem, hrecv_sem,
):
    nx, ny, nz, blocks, cap, cx = sizes
    slots = nx * cap
    gx, gy, gz = lax.axis_index("gx"), lax.axis_index("gy"), lax.axis_index("gz")
    right, left = lax.rem(gx + 1, nx), lax.rem(gx + nx - 1, nx)
    up, down = lax.rem(gy + 1, ny), lax.rem(gy + ny - 1, ny)
    other = lax.rem(gz + 1, nz)

    def fetch(source, target, n):
        copy = pltpu.make_async_copy(source, target, hsend_sem.at[n])
        copy.start()
        return copy

    small = [
        fetch(source, target, n)
        for n, (source, target) in enumerate(
            ((pcol_hbm, pcol), (mpos_hbm, mpos), (moff_hbm, moff), (links_hbm, links))
        )
    ]
    barrier = pltpu.get_barrier_semaphore()
    near = [(a, b, gz) for a in (right, left) for b in (up, down)]
    near += [(right, gy, other), (left, gy, other)]
    for o in range(1, nx):
        near.append((lax.rem(gx + o, nx), gy, gz))
    near += [(gx, up, other), (gx, down, other), (gx, up, gz), (gx, down, gz), (gx, gy, other)]
    for device in near:
        pl.semaphore_signal(barrier, inc=1, device_id=device, device_id_type=MESH)
    rims = [
        fetch(pop_hbm.at[:, pl.ds(0, 1)], pop.at[:, pl.ds(0, 1)], 4),
        fetch(pop_hbm.at[:, pl.ds(cx - 1, 1)], pop.at[:, pl.ds(cx - 1, 1)], 5),
        fetch(solid_hbm, solid, 6),
    ]
    core = fetch(pop_hbm.at[:, pl.ds(1, cx - 2)], pop.at[:, pl.ds(1, cx - 2)], 8)

    row = lax.broadcasted_iota(jnp.int32, (8, 128), 0)
    lane = lax.broadcasted_iota(jnp.int32, (8, 128), 1)

    for copy in small:
        copy.wait()
    named = [jnp.broadcast_to(pcol[:, b : b + 1], (8, 128)) for b in range(blocks)]
    spots = []
    for b in range(blocks):
        spot = named[b] * cap
        for e in range(b):
            spot = spot + jnp.where(named[e] == named[b], 1, 0)
        spots.append(spot)
        where_to[b] = spot
    tiles = []
    for b in range(blocks):
        tiles.append(
            jnp.concatenate(
                [mpos[k, b : b + 1, :] for k in range(3)]
                + [moff[k, b : b + 1, :] for k in range(3)]
                + [links[b].astype(jnp.float32)],
                axis=0,
            )
        )
    empty = jnp.where(row < 3, PARK, 0.0)
    for s in range(slots):
        tile = empty
        for b in range(blocks):
            tile = jnp.where(spots[b] == s, tiles[b], tile)
        g, c = s // cap, s % cap
        msend[g, 6 * c : 6 * c + 6, :] = tile[0:6, :]
        lsend[g, 2 * c : 2 * c + 2, :] = tile[6:8, :]

    pl.semaphore_wait(barrier, len(near))

    peers = []
    low, high = gx * 0, gx * 0 + (nx - 1)
    for _ in range(nx - 1):
        far = jnp.where(high - gx > gx - low, 1, 0)
        peers.append(far * high + (1 - far) * low)
        low, high = low + (1 - far), high - far

    origins = [gx] + peers[::-1]

    def exchange(source, target, rows, send_sem, recv_sem):
        copies = []
        for to in peers:
            copy = pltpu.make_async_remote_copy(
                src_ref=source.at[to, pl.ds(0, rows)],
                dst_ref=target.at[gx, pl.ds(0, rows)],
                send_sem=send_sem.at[to],
                recv_sem=recv_sem.at[gx],
                device_id=(to, gy, gz),
                device_id_type=MESH,
            )
            copy.start()
            copies.append(copy)
        target[gx, 0:rows, :] = source[gx, 0:rows, :]
        return copies

    def arrive(source, target, rows, send_sem, recv_sem, origin):
        pltpu.make_async_remote_copy(
            src_ref=source.at[origin, pl.ds(0, rows)],
            dst_ref=target.at[origin, pl.ds(0, rows)],
            send_sem=send_sem.at[origin],
            recv_sem=recv_sem.at[origin],
            device_id=(origin, gy, gz),
            device_id_type=MESH,
        ).wait_recv()

    places = (msend, mrecv, 6 * cap, csend_sem.at[0], mrecv_sem)
    tethers = (lsend, lrecv, 2 * cap, csend_sem.at[1], lrecv_sem)
    returns = (dsend, dback, 3 * cap, csend_sem.at[0], brecv_sem)
    place_copies = exchange(*places)
    for g in range(nx):
        mrecv[g, 6 * cap : 6 * cap + 2, :] = jnp.zeros((2, 128), jnp.float32)

    def sender(step, base):
        copies = []

        def go(source, target, device, n=None):
            n = base + len(copies) if n is None else n
            copy = pltpu.make_async_remote_copy(
                src_ref=source,
                dst_ref=target,
                send_sem=hsend_sem.at[n],
                recv_sem=hrecv_sem.at[step % 2, n],
                device_id=device,
                device_id_type=MESH,
            )
            copy.start()
            copies.append(copy)

        return go, copies

    def halo_x(step):
        go, copies = sender(step, 0)
        z = zsend.at[step, 0]
        lead = jnp.where(gx == 0, 1, 0)
        for d in (lead, 1 - lead):
            x, a = (1 - d) * (cx - 1), d * left + (1 - d) * right
            for turn, b in enumerate((up, down)):
                go(
                    ysend.at[step, turn, 1 + d, pl.ds(x, 1)],
                    yhalo.at[step, turn, 1 + d, pl.ds(cx, 1)],
                    (a, b, gz),
                    4 * d + turn,
                )
            go(z, zhalo.at[step, 1 + d], (a, gy, other), 4 * d + 2)
            q = pl.ds(9 + 5 * d, 5)
            go(post.at[step, q, x + 1], post.at[step, q, d * (cx + 1)], (a, gy, gz), 4 * d + 3)
        return copies

    def halo_yz(step):
        go, copies = sender(step, 8)
        z = zsend.at[step, 1]
        go(z, zhalo.at[step, 3], (gx, up, other))
        go(z, zhalo.at[step, 4], (gx, down, other))
        go(ysend.at[step, 0], yhalo.at[step, 0, :, pl.ds(0, cx)], (gx, up, gz))
        go(ysend.at[step, 1], yhalo.at[step, 1, :, pl.ds(0, cx)], (gx, down, gz))
        go(z, zhalo.at[step, 0], (gx, gy, other))
        return copies

    def over_edges(body, carry):
        return lax.fori_loop(0, 2, lambda i, c: body(i * (cx - 1), c), carry, unroll=2)

    def over_middle(body, carry):
        return lax.fori_loop(1, cx - 1, body, carry, unroll=cx - 2)

    def emit(step, x, values):
        for q in range(19):
            post[step, PLACE[q], x + 1] = values[q]

    def rim(step, x, values, packed):
        for d, edge in ((0, 7), (1, 0)):
            for j, q in enumerate(Y_MOVERS[d]):
                ysend[step, d, j, pl.ds(x, 1)] = values[q][edge : edge + 1, :]
        for d, edge in ((0, 127), (1, 0)):
            for j, q in enumerate(Z_MOVERS[d]):
                column = jnp.broadcast_to(values[q][:, edge : edge + 1], (8, 128))
                packed = jnp.where(lane == x + (d * HALF + j * 8), column, packed)
        return packed

    def stream(step, x):
        turned = pltpu.roll(zin[...], lax.rem(128 - x, 128), axis=1)
        f = []
        for q in range(19):
            c = VELOCITY[q]
            tile = post[step, PLACE[q], x + 1 - c[0]]
            if c[1]:
                d = 0 if c[1] == 1 else 1
                j = Y_MOVERS[d].index(q)
                if c[0] == 1:
                    at = lax.rem(x + cx, cx + 1)
                else:
                    at = x - c[0]
                line = jnp.broadcast_to(yhalo[step, d, j, pl.ds(at, 1)], (8, 128))
                tile = jnp.where(row == (0 if d == 0 else 7), line, pltpu.roll(tile, 1 if d == 0 else 7, axis=0))
            if c[2]:
                d = 0 if c[2] == 1 else 1
                j = Z_MOVERS[d].index(q)
                k = d * HALF + j * 8
                column = jnp.broadcast_to(turned[:, k : k + 1], (8, 128))
                tile = jnp.where(
                    lane == (0 if d == 0 else 127), column, pltpu.roll(tile, 1 if d == 0 else 127, axis=1)
                )
            f.append(tile)
            outf[q, x] = tile
        density, momentum = moments(f)
        mom[0, x] = density
        over = 1.0 / density
        for k in range(3):
            mom[k + 1, x] = momentum[k]
            vfield[k, x] = momentum[k] * over

    def combine(step, whole):
        face = zhalo[step, 0]
        group = lax.rem(lane, HALF) // 8
        inside = lax.rem(lane, 8)
        forward = pltpu.roll(face, 1, axis=1)
        backward = pltpu.roll(face, 127, axis=1)
        if whole:
            forward = jnp.where(inside == 0, pltpu.roll(zhalo[step, 1], 121, axis=1), forward)
            backward = jnp.where(inside == 7, pltpu.roll(zhalo[step, 2], 7, axis=1), backward)
        rising = jnp.where(
            row == 0, pltpu.roll(zhalo[step, 3], 1, axis=0), pltpu.roll(face, 1, axis=0)
        )
        falling = jnp.where(
            row == 7, pltpu.roll(zhalo[step, 4], 7, axis=0), pltpu.roll(face, 7, axis=0)
        )
        zin[...] = jnp.where(
            group == 0,
            face,
            jnp.where(
                group == 1,
                forward,
                jnp.where(group == 2, backward, jnp.where(group == 3, rising, falling)),
            ),
        )

    edges = (0, cx - 1)
    middle = tuple(range(1, cx - 1))
    inner = tuple(range(2, cx - 2))

    def spread(step, xs, fresh, terms, plane):
        size = len(xs) * 8
        n = 3 * size
        f32, bf16 = jnp.float32, jnp.bfloat16
        level = lax.broadcasted_iota(jnp.int32, (128, 256), 0).astype(f32)
        depth, ahead = level.astype(bf16), (level - 1.0).astype(bf16)
        cell = lax.broadcasted_iota(jnp.int32, (8, 256), 0).astype(f32)

        def spanned(values, k):
            return jnp.broadcast_to(values[k : k + 1, :], (128, 256)).astype(bf16)

        def one(turn, h):
            g = origins[turn]
            i = turn * (cap // 2) + h
            info = jnp.concatenate([mrecv[g, pl.ds(6 * (2 * h + e), 8), :] for e in range(2)], axis=1)
            if step == 0:
                position = info
                disp[i] = jnp.zeros((8, 256), f32)
            else:
                shift = disp[i]
                position = info + shift
            at = pl.ds(i * 256, 256)
            if fresh:
                force = K_TETHER * ((info + pltpu.roll(info, 5, axis=0)) - position)
                if step > 0:
                    for k in range(2):
                        chosen = jnp.concatenate(
                            [
                                jnp.take_along_axis(
                                    shift[:, e * 128 : e * 128 + 128],
                                    jnp.broadcast_to(lrecv[g, pl.ds(2 * (2 * h + e) + k, 1), :], (8, 128)).astype(jnp.int32),
                                    axis=1,
                                )
                                for e in range(2)
                            ],
                            axis=1,
                        )
                        force = force + K_SPRING * (chosen - shift)
                    pull[i] = force
                floor = jnp.floor(position)
                above = position - floor
                below = 1.0 - above
                under = spanned(floor, 2)
                at_next, at_floor = ahead == under, depth == under
                nothing = jnp.zeros((128, 256), bf16)
                below_rest = below - below.astype(bf16).astype(f32)
                above_rest = above - above.astype(bf16).astype(f32)
                highs = jnp.where(at_next, spanned(above, 2), nothing)
                lows = jnp.where(at_next, spanned(above_rest, 2), nothing)
                pz[0:128, at] = jnp.where(at_floor, spanned(below, 2), highs)
                pz[128:256, at] = jnp.where(at_floor, spanned(below_rest, 2), lows)
            else:
                force = pull[i]
            wx = jnp.maximum(0.0, 1.0 - jnp.abs(position[0:1, :] - cell))
            wy = jnp.maximum(0.0, 1.0 - jnp.abs(position[1:2, :] - cell))
            full = jnp.concatenate([wx[x : x + 1, :] * wy for x in xs], axis=0)
            plane[0:size, at] = full
            for k in range(3):
                term = force[k : k + 1, :] * full
                high = term.astype(bf16)
                terms[k * size : k * size + size, at] = high
                terms[n + k * size : n + k * size + size, at] = (term - high.astype(f32)).astype(bf16)

        def gather(at):
            product = lax.dot_general(
                terms[0 : 2 * n, at], pz[:, at], (((1,), (1,)), ((), ())), preferred_element_type=f32
            )
            return product[0:n, 0:128] + (product[0:n, 128:256] + product[n : 2 * n, 0:128])

        total = None
        for turn in range(nx):
            if step == 0 and turn:
                arrive(*places, origins[turn])
            for h in range(cap // 2):
                one(turn, h)
            if step == 0:
                part = gather(pl.ds(turn * (cap * 128), cap * 128))
                total = part if total is None else total + part
        if step > 0:
            for h in range(4):
                part = gather(pl.ds(h * slots * 32, slots * 32))
                total = part if total is None else total + part
        for k in range(3):
            for i, x in enumerate(xs):
                gfield[k, x] = total[k * size + i * 8 : k * size + i * 8 + 8]

    def sample(xs, vsplit, plane):
        size = len(xs) * 8
        n = 3 * size
        v = jnp.concatenate([vfield[k, x] for k in range(3) for x in xs], axis=0)
        high = v.astype(jnp.bfloat16)
        low = (v - high.astype(jnp.float32)).astype(jnp.bfloat16)
        vsplit[0:n, 0:128] = high
        vsplit[0:n, 128:256] = high
        vsplit[n : 2 * n, 0:128] = low
        vsplit[n : 2 * n, 128:256] = low
        for i in range(slots * 128 // WIDE):
            at = pl.ds(i * WIDE, WIDE)
            product = jnp.dot(vsplit[0 : 2 * n], pz[:, at], preferred_element_type=jnp.float32)
            full = plane[0:size, at]
            for k in range(3):
                part = product[k * size : k * size + size] + product[n + k * size : n + k * size + size]
                moved = jnp.sum(part * full, axis=0, keepdims=True)
                for h in range(WIDE // 256):
                    pair = i * (WIDE // 256) + h
                    disp[pair, k : k + 1, :] = (
                        disp[pair, k : k + 1, :] + moved[:, h * 256 : h * 256 + 256]
                    )

    def first(x, packed):
        f = [pop[q, x] for q in range(19)]
        density, momentum = moments(f)
        mom[0, x] = density
        for k in range(3):
            mom[k + 1, x] = momentum[k]
        values = collide(f, density, momentum, None, solid[x] == 1)
        emit(0, x, values)
        return rim(0, x, values, packed)

    def coupled(step):
        def body(x, packed):
            f = [outf[q, x] for q in range(19)]
            values = collide(
                f, mom[0, x], [mom[k, x] for k in range(1, 4)],
                [gfield[k, x] for k in range(3)], solid[x] == 1,
            )
            emit(step, x, values)
            return rim(step, x, values, packed)

        return body

    def driven(x, carry):
        f = [pop[q, x] for q in range(19)]
        values = collide(
            f, mom[0, x], [mom[k, x] for k in range(1, 4)], [gfield[k, x] for k in range(3)],
            solid[x] == 1,
        )
        emit(0, x, values)
        return carry

    def moving(step):
        def body(x, carry):
            stream(step, x)
            return carry

        return body

    for copy in rims:
        copy.wait()
    packed = over_edges(first, jnp.zeros((8, 128), jnp.float32))
    zsend[0, 0] = packed
    x_halos = [halo_x(0)]
    core.wait()
    zsend[0, 1] = over_middle(first, packed)
    yz_halos = [halo_yz(0)]
    link_copies = exchange(*tethers)
    spread(0, inner, True, mid_terms, mid_plane)
    lax.fori_loop(2, cx - 2, driven, 0, unroll=cx - 4)

    for step in range(STEPS):
        last = step == STEPS - 1
        for copy in yz_halos[step]:
            copy.wait_recv()
        combine(step, False)
        over_middle(moving(step), 0)
        sample(inner if step == 0 else middle, vmid, mid_plane)
        if step == 0:
            for g in peers[::-1]:
                arrive(*tethers, g)
            spread(1, edges, True, edge_terms, edge_plane)
        for copy in x_halos[step]:
            copy.wait_recv()
        combine(step, True)
        over_edges(moving(step), 0)
        if step > 0:
            sample(edges, vedge, edge_plane)
        if last:
            break
        if step > 0:
            spread(step + 1, edges, True, edge_terms, edge_plane)
        packed = over_edges(coupled(step + 1), jnp.zeros((8, 128), jnp.float32))
        zsend[step + 1, 0] = packed
        for copy in x_halos[step]:
            copy.wait_send()
        x_halos.append(halo_x(step + 1))
        spread(step + 1, middle, False, mid_terms, mid_plane)
        zsend[step + 1, 1] = over_middle(coupled(step + 1), packed)
        for copy in yz_halos[step]:
            copy.wait_send()
        yz_halos.append(halo_yz(step + 1))

    for copy in place_copies:
        copy.wait_send()
    for c in range(slots):
        h = (c % 2) * 128
        at = 3 * (c % cap)
        dsend[origins[c // cap], at : at + 3, :] = disp[c // 2, 0:3, h : h + 128]
    back_copies = exchange(*returns)
    for copies in [link_copies, x_halos[-1], yz_halos[-1]]:
        for copy in copies:
            copy.wait_send()
    for g in peers[::-1]:
        arrive(*returns, g)
    tiles = [jnp.zeros((3, 128), jnp.float32) for b in range(blocks)]
    for c in range(slots):
        at = 3 * (c % cap)
        came = dback[c // cap, at : at + 3, :]
        tiles = [jnp.where(where_to[b, 0:3, :] == c, came, tiles[b]) for b in range(blocks)]
    for b in range(blocks):
        for k in range(3):
            outs[k, b : b + 1, :] = tiles[b][k : k + 1, :]
    for copy in back_copies:
        copy.wait_send()


def flush(new, shift, new_out, shift_out, a_sem, b_sem):
    a = pltpu.make_async_copy(new, new_out, a_sem)
    b = pltpu.make_async_copy(shift, shift_out, b_sem)
    a.start()
    b.start()
    a.wait()
    b.wait()


def shards(sizes, populations, solid, marker_pos, anchor_offset, links, patch_col):
    nx, ny, nz, blocks, cap, cx = sizes
    slots = nx * cap
    f32 = jnp.float32
    tile = (8, 128)
    mid = 8 * (cx - 2)
    padded = lambda rows: -(-rows // 8) * 8
    dma = pltpu.SemaphoreType.DMA
    new, shift = pl.pallas_call(
        functools.partial(kernel, sizes),
        out_shape=(
            pltpu.VMEM(populations.shape, f32),
            pltpu.VMEM((3, blocks, 128), f32),
        ),
        in_specs=[pl.BlockSpec(memory_space=pltpu.HBM)] * 6,
        scratch_shapes=[
            pltpu.VMEM(populations.shape, f32),
            pltpu.VMEM(solid.shape, jnp.int32),
            pltpu.VMEM((3, blocks, 128), f32),
            pltpu.VMEM((3, blocks, 128), f32),
            pltpu.VMEM(links.shape, jnp.int32),
            pltpu.VMEM((1, blocks), jnp.int32),
            pltpu.VMEM((STEPS, 19, cx + 2) + tile, f32),
            pltpu.VMEM((STEPS, 2, 5) + tile, f32),
            pltpu.VMEM((STEPS, 2, 5, 16, 128), f32),
            pltpu.VMEM((STEPS, 2) + tile, f32),
            pltpu.VMEM((STEPS, 5) + tile, f32),
            pltpu.VMEM(tile, f32),
            pltpu.VMEM((4, cx) + tile, f32),
            pltpu.VMEM((3, cx) + tile, f32),
            pltpu.VMEM((3, cx) + tile, f32),
            pltpu.VMEM((96, 256), jnp.bfloat16),
            pltpu.VMEM((6 * mid, 256), jnp.bfloat16),
            pltpu.VMEM((slots // 2, 8, 256), f32),
            pltpu.VMEM((nx, padded(6 * cap), 128), f32),
            pltpu.VMEM((nx, padded(6 * cap + 2), 128), f32),
            pltpu.VMEM((nx, padded(2 * cap), 128), f32),
            pltpu.VMEM((nx, padded(2 * cap), 128), f32),
            pltpu.VMEM((slots // 2, 8, 256), f32),
            pltpu.VMEM((nx, padded(3 * cap), 128), f32),
            pltpu.VMEM((nx, padded(3 * cap), 128), f32),
            pltpu.VMEM((blocks,) + tile, jnp.int32),
            pltpu.VMEM((96, slots * 128), jnp.bfloat16),
            pltpu.VMEM((6 * mid, slots * 128), jnp.bfloat16),
            pltpu.VMEM((256, slots * 128), jnp.bfloat16),
            pltpu.VMEM((16, slots * 128), f32),
            pltpu.VMEM((mid, slots * 128), f32),
            dma((2, nx)), dma((nx,)), dma((nx,)), dma((nx,)),
            dma((13,)), dma((2, 13)),
        ],
        compiler_params=pltpu.CompilerParams(
            collective_id=0, has_side_effects=True, vmem_limit_bytes=62 * 1024 * 1024
        ),
    )(
        populations,
        solid,
        jnp.transpose(marker_pos, (1, 0, 2)),
        jnp.transpose(anchor_offset, (1, 0, 2)),
        links,
        patch_col.T,
    )
    new, shift = pl.pallas_call(
        flush,
        out_shape=(
            jax.ShapeDtypeStruct(populations.shape, f32),
            jax.ShapeDtypeStruct((3, blocks, 128), f32),
        ),
        in_specs=[pl.BlockSpec(memory_space=pltpu.VMEM)] * 2,
        out_specs=(pl.BlockSpec(memory_space=pltpu.HBM),) * 2,
        scratch_shapes=[dma, dma],
    )(pltpu.with_memory_space_constraint(new, pltpu.VMEM), pltpu.with_memory_space_constraint(shift, pltpu.VMEM))
    return new, jnp.transpose(shift, (1, 0, 2))


def solution(mesh):
    placed = (
        P(None, "gx", "gy", "gz"),
        P("gx", "gy", "gz"),
        P(("gx", "gy", "gz"), None, None),
        P(("gx", "gy", "gz"), None, None),
        P(("gx", "gy", "gz"), None, None),
        P(("gx", "gy", "gz"), None),
    )

    def whole(populations, solid, marker_pos, anchor_offset, links, patch_col):
        nx, ny, nz = (mesh.shape[name] for name in ("gx", "gy", "gz"))
        blocks = marker_pos.shape[0] // (nx * ny * nz)
        cap = max(2, 2 * blocks // nx)
        sizes = (nx, ny, nz, blocks, cap, populations.shape[1] // nx)
        return jax.shard_map(
            functools.partial(shards, sizes),
            mesh=mesh,
            in_specs=placed,
            out_specs=(P(None, "gx", "gy", "gz"), P(("gx", "gy", "gz"), None, None)),
            check_vma=False,
        )(populations, solid, marker_pos, anchor_offset, links, patch_col)

    return whole
```

```python
import functools

import jax
import jax.numpy as jnp
from jax import lax
from jax.experimental import pallas as pl
from jax.experimental.pallas import tpu as pltpu
from jax.sharding import PartitionSpec as P

STEPS = 3
VELOCITY = (
    (0, 0, 0), (1, 0, 0), (-1, 0, 0), (0, 1, 0), (0, -1, 0), (0, 0, 1), (0, 0, -1),
    (1, 1, 0), (-1, -1, 0), (1, -1, 0), (-1, 1, 0), (1, 0, 1), (-1, 0, -1), (1, 0, -1),
    (-1, 0, 1), (0, 1, 1), (0, -1, -1), (0, 1, -1), (0, -1, 1),
)
WEIGHTS = (1.0 / 3.0,) + (1.0 / 18.0,) * 6 + (1.0 / 36.0,) * 12
OPPOSITE = (0, 2, 1, 4, 3, 6, 5, 8, 7, 10, 9, 12, 11, 14, 13, 16, 15, 18, 17)
TAU = 0.8
K_TETHER = 0.05
K_SPRING = 0.1
NUMBER = {c: q for q, c in enumerate(VELOCITY)}
ORDER = (
    [q for q in range(19) if VELOCITY[q][0] == 0]
    + [q for q in range(19) if VELOCITY[q][0] == 1]
    + [q for q in range(19) if VELOCITY[q][0] == -1]
)
PLACE = {q: i for i, q in enumerate(ORDER)}
Y_MOVERS = [
    [NUMBER[(0, s, 0)], NUMBER[(1, s, 0)], NUMBER[(-1, s, 0)], NUMBER[(0, s, 1)], NUMBER[(0, s, -1)]]
    for s in (1, -1)
]
Z_MOVERS = [
    [NUMBER[(0, 0, s)], NUMBER[(1, 0, s)], NUMBER[(-1, 0, s)], NUMBER[(0, 1, s)], NUMBER[(0, -1, s)]]
    for s in (1, -1)
]
MESH = pl.DeviceIdType.MESH
PARK = -1000.0
CELL_UNROLL = 8
WIDE = 1024
HALF = 64


def axis_sum(values, column):
    total = None
    for q in range(19):
        sign = VELOCITY[q][column]
        if sign == 0:
            continue
        term = values[q]
        total = (term if sign == 1 else -term) if total is None else (
            total + term if sign == 1 else total - term
        )
    return total


def moments(f):
    density = f[0]
    for q in range(1, 19):
        density = density + f[q]
    return density, [axis_sum(f, column) for column in range(3)]


def project(vector, direction):
    total = None
    for column in range(3):
        if direction[column]:
            term = vector[column] if direction[column] == 1 else -vector[column]
            total = term if total is None else total + term
    return total


def collide(f, density, momentum, field, wall):
    over = 1.0 / density
    omega = 1.0 / TAU
    factor = 1.0 - 0.5 / TAU
    if field is None:
        u = [momentum[k] * over for k in range(3)]
    else:
        u = [(momentum[k] + 0.5 * field[k]) * over for k in range(3)]
    square = u[0] * u[0] + u[1] * u[1] + u[2] * u[2]
    base = omega * density * (1.0 - 1.5 * square)
    if field is not None:
        power = u[0] * field[0] + u[1] * field[1] + u[2] * field[2]
        base = base - (3.0 * factor) * power
    post = [None] * 19
    rest = (1.0 - omega) * f[0] + WEIGHTS[0] * base
    post[0] = jnp.where(wall, f[0], rest)
    for numbers in (range(1, 7, 2), range(7, 19, 2)):
        weight = WEIGHTS[numbers[0]]
        level = weight * base
        scaled = (4.5 * weight * omega) * density
        if field is not None:
            push = [(4.5 * factor * weight) * field[k] for k in range(3)]
        for q in numbers:
            p = OPPOSITE[q]
            along = project(u, VELOCITY[q])
            flow = scaled * along
            if field is None:
                odd = (2.0 / 3.0) * flow
                even = level + along * flow
            else:
                pushed = project(push, VELOCITY[q])
                flow = flow + pushed
                odd = (2.0 / 3.0) * flow
                even = level + along * (flow + pushed)
            post[q] = jnp.where(wall, f[p], (1.0 - omega) * f[q] + (even + odd))
            post[p] = jnp.where(wall, f[q], (1.0 - omega) * f[p] + (even - odd))
    return post


def kernel(
    sizes,
    pop_hbm, solid_hbm, mpos_hbm, moff_hbm, links_hbm, pcol_hbm,
    outf, outs,
    pop, solid, mpos, moff, links, pcol,
    post, ysend, yhalo, zsend, zhalo, zin, mom, gfield, vfield,
    vedge, vmid, pull,
    msend, mrecv, lsend, lrecv, disp, dsend, dback, where_to,
    edge_terms, mid_terms, pz, edge_plane, mid_plane,
    csend_sem, mrecv_sem, lrecv_sem, brecv_sem, hsend_sem, hrecv_sem,
):
    nx, ny, nz, blocks, cap, cx = sizes
    slots = nx * cap
    gx, gy, gz = lax.axis_index("gx"), lax.axis_index("gy"), lax.axis_index("gz")
    right, left = lax.rem(gx + 1, nx), lax.rem(gx + nx - 1, nx)
    up, down = lax.rem(gy + 1, ny), lax.rem(gy + ny - 1, ny)
    other = lax.rem(gz + 1, nz)

    def fetch(source, target, n):
        copy = pltpu.make_async_copy(source, target, hsend_sem.at[n])
        copy.start()
        return copy

    small = [
        fetch(source, target, n)
        for n, (source, target) in enumerate(
            ((pcol_hbm, pcol), (mpos_hbm, mpos), (moff_hbm, moff), (links_hbm, links))
        )
    ]
    barrier = pltpu.get_barrier_semaphore()
    near = [(a, b, gz) for a in (right, left) for b in (up, down)]
    near += [(right, gy, other), (left, gy, other)]
    for o in range(1, nx):
        near.append((lax.rem(gx + o, nx), gy, gz))
    near += [(gx, up, other), (gx, down, other), (gx, up, gz), (gx, down, gz), (gx, gy, other)]
    for device in near:
        pl.semaphore_signal(barrier, inc=1, device_id=device, device_id_type=MESH)
    rims = [
        fetch(pop_hbm.at[:, pl.ds(0, 1)], pop.at[:, pl.ds(0, 1)], 4),
        fetch(pop_hbm.at[:, pl.ds(cx - 1, 1)], pop.at[:, pl.ds(cx - 1, 1)], 5),
        fetch(solid_hbm, solid, 6),
    ]
    core = fetch(pop_hbm.at[:, pl.ds(1, cx - 2)], pop.at[:, pl.ds(1, cx - 2)], 8)

    row = lax.broadcasted_iota(jnp.int32, (8, 128), 0)
    lane = lax.broadcasted_iota(jnp.int32, (8, 128), 1)

    for copy in small:
        copy.wait()
    named = [jnp.broadcast_to(pcol[:, b : b + 1], (8, 128)) for b in range(blocks)]
    spots = []
    for b in range(blocks):
        spot = named[b] * cap
        for e in range(b):
            spot = spot + jnp.where(named[e] == named[b], 1, 0)
        spots.append(spot)
        where_to[b] = spot
    tiles = []
    for b in range(blocks):
        tiles.append(
            jnp.concatenate(
                [mpos[k, b : b + 1, :] for k in range(3)]
                + [moff[k, b : b + 1, :] for k in range(3)]
                + [links[b].astype(jnp.float32)],
                axis=0,
            )
        )
    empty = jnp.where(row < 3, PARK, 0.0)
    for s in range(slots):
        tile = empty
        for b in range(blocks):
            tile = jnp.where(spots[b] == s, tiles[b], tile)
        g, c = s // cap, s % cap
        msend[g, 6 * c : 6 * c + 6, :] = tile[0:6, :]
        lsend[g, 2 * c : 2 * c + 2, :] = tile[6:8, :]

    pl.semaphore_wait(barrier, len(near))

    peers = []
    low, high = gx * 0, gx * 0 + (nx - 1)
    for _ in range(nx - 1):
        far = jnp.where(high - gx > gx - low, 1, 0)
        peers.append(far * high + (1 - far) * low)
        low, high = low + (1 - far), high - far

    origins = [gx] + peers[::-1]

    def exchange(source, target, rows, send_sem, recv_sem):
        copies = []
        for to in peers:
            copy = pltpu.make_async_remote_copy(
                src_ref=source.at[to, pl.ds(0, rows)],
                dst_ref=target.at[gx, pl.ds(0, rows)],
                send_sem=send_sem.at[to],
                recv_sem=recv_sem.at[gx],
                device_id=(to, gy, gz),
                device_id_type=MESH,
            )
            copy.start()
            copies.append(copy)
        target[gx, 0:rows, :] = source[gx, 0:rows, :]
        return copies

    def arrive(source, target, rows, send_sem, recv_sem, origin):
        pltpu.make_async_remote_copy(
            src_ref=source.at[origin, pl.ds(0, rows)],
            dst_ref=target.at[origin, pl.ds(0, rows)],
            send_sem=send_sem.at[origin],
            recv_sem=recv_sem.at[origin],
            device_id=(origin, gy, gz),
            device_id_type=MESH,
        ).wait_recv()

    places = (msend, mrecv, 6 * cap, csend_sem.at[0], mrecv_sem)
    tethers = (lsend, lrecv, 2 * cap, csend_sem.at[1], lrecv_sem)
    returns = (dsend, dback, 3 * cap, csend_sem.at[0], brecv_sem)
    place_copies = exchange(*places)
    for g in range(nx):
        mrecv[g, 6 * cap : 6 * cap + 2, :] = jnp.zeros((2, 128), jnp.float32)

    def sender(step, base):
        copies = []

        def go(source, target, device, n=None):
            n = base + len(copies) if n is None else n
            copy = pltpu.make_async_remote_copy(
                src_ref=source,
                dst_ref=target,
                send_sem=hsend_sem.at[n],
                recv_sem=hrecv_sem.at[step % 2, n],
                device_id=device,
                device_id_type=MESH,
            )
            copy.start()
            copies.append(copy)

        return go, copies

    def halo_x(step):
        go, copies = sender(step, 0)
        z = zsend.at[step, 0]
        lead = jnp.where(gx == 0, 1, 0)
        for d in (lead, 1 - lead):
            x, a = (1 - d) * (cx - 1), d * left + (1 - d) * right
            for turn, b in enumerate((up, down)):
                go(
                    ysend.at[step, turn, 1 + d, pl.ds(x, 1)],
                    yhalo.at[step, turn, 1 + d, pl.ds(cx, 1)],
                    (a, b, gz),
                    4 * d + turn,
                )
            go(z, zhalo.at[step, 1 + d], (a, gy, other), 4 * d + 2)
            q = pl.ds(9 + 5 * d, 5)
            go(post.at[step, q, x + 1], post.at[step, q, d * (cx + 1)], (a, gy, gz), 4 * d + 3)
        return copies

    def halo_yz(step):
        go, copies = sender(step, 8)
        z = zsend.at[step, 1]
        go(z, zhalo.at[step, 3], (gx, up, other))
        go(z, zhalo.at[step, 4], (gx, down, other))
        go(z, zhalo.at[step, 0], (gx, gy, other))
        go(ysend.at[step, 0], yhalo.at[step, 0, :, pl.ds(0, cx)], (gx, up, gz))
        go(ysend.at[step, 1], yhalo.at[step, 1, :, pl.ds(0, cx)], (gx, down, gz))
        return copies

    def over_edges(body, carry):
        return lax.fori_loop(0, 2, lambda i, c: body(i * (cx - 1), c), carry, unroll=2)

    def over_middle(body, carry):
        return lax.fori_loop(1, cx - 1, body, carry, unroll=cx - 2)

    def emit(step, x, values):
        for q in range(19):
            post[step, PLACE[q], x + 1] = values[q]

    def rim(step, x, values, packed):
        for d, edge in ((0, 7), (1, 0)):
            for j, q in enumerate(Y_MOVERS[d]):
                ysend[step, d, j, pl.ds(x, 1)] = values[q][edge : edge + 1, :]
        for d, edge in ((0, 127), (1, 0)):
            for j, q in enumerate(Z_MOVERS[d]):
                column = jnp.broadcast_to(values[q][:, edge : edge + 1], (8, 128))
                packed = jnp.where(lane == x + (d * HALF + j * 8), column, packed)
        return packed

    def stream(step, x):
        turned = pltpu.roll(zin[...], lax.rem(128 - x, 128), axis=1)
        f = []
        for q in range(19):
            c = VELOCITY[q]
            tile = post[step, PLACE[q], x + 1 - c[0]]
            if c[1]:
                d = 0 if c[1] == 1 else 1
                j = Y_MOVERS[d].index(q)
                if c[0] == 1:
                    at = lax.rem(x + cx, cx + 1)
                else:
                    at = x - c[0]
                line = jnp.broadcast_to(yhalo[step, d, j, pl.ds(at, 1)], (8, 128))
                tile = jnp.where(row == (0 if d == 0 else 7), line, pltpu.roll(tile, 1 if d == 0 else 7, axis=0))
            if c[2]:
                d = 0 if c[2] == 1 else 1
                j = Z_MOVERS[d].index(q)
                k = d * HALF + j * 8
                column = jnp.broadcast_to(turned[:, k : k + 1], (8, 128))
                tile = jnp.where(
                    lane == (0 if d == 0 else 127), column, pltpu.roll(tile, 1 if d == 0 else 127, axis=1)
                )
            f.append(tile)
            outf[q, x] = tile
        density, momentum = moments(f)
        mom[0, x] = density
        over = 1.0 / density
        for k in range(3):
            mom[k + 1, x] = momentum[k]
            vfield[k, x] = momentum[k] * over

    def combine(step, whole):
        face = zhalo[step, 0]
        group = lax.rem(lane, HALF) // 8
        inside = lax.rem(lane, 8)
        forward = pltpu.roll(face, 1, axis=1)
        backward = pltpu.roll(face, 127, axis=1)
        if whole:
            forward = jnp.where(inside == 0, pltpu.roll(zhalo[step, 1], 121, axis=1), forward)
            backward = jnp.where(inside == 7, pltpu.roll(zhalo[step, 2], 7, axis=1), backward)
        rising = jnp.where(
            row == 0, pltpu.roll(zhalo[step, 3], 1, axis=0), pltpu.roll(face, 1, axis=0)
        )
        falling = jnp.where(
            row == 7, pltpu.roll(zhalo[step, 4], 7, axis=0), pltpu.roll(face, 7, axis=0)
        )
        zin[...] = jnp.where(
            group == 0,
            face,
            jnp.where(
                group == 1,
                forward,
                jnp.where(group == 2, backward, jnp.where(group == 3, rising, falling)),
            ),
        )

    edges = (0, cx - 1)
    middle = tuple(range(1, cx - 1))
    inner = tuple(range(2, cx - 2))

    def spread(step, xs, fresh, terms, plane):
        size = len(xs) * 8
        n = 3 * size
        f32, bf16 = jnp.float32, jnp.bfloat16
        level = lax.broadcasted_iota(jnp.int32, (128, 256), 0).astype(f32)
        depth, ahead = level.astype(bf16), (level - 1.0).astype(bf16)
        cell = lax.broadcasted_iota(jnp.int32, (8, 256), 0).astype(f32)

        def spanned(values, k):
            return jnp.broadcast_to(values[k : k + 1, :], (128, 256)).astype(bf16)

        def one(turn, h):
            g = origins[turn]
            i = turn * (cap // 2) + h
            info = jnp.concatenate([mrecv[g, pl.ds(6 * (2 * h + e), 8), :] for e in range(2)], axis=1)
            if step == 0:
                position = info
                disp[i] = jnp.zeros((8, 256), f32)
            else:
                shift = disp[i]
                position = info + shift
            at = pl.ds(i * 256, 256)
            if fresh:
                force = K_TETHER * ((info + pltpu.roll(info, 5, axis=0)) - position)
                if step > 0:
                    for k in range(2):
                        chosen = jnp.concatenate(
                            [
                                jnp.take_along_axis(
                                    shift[:, e * 128 : e * 128 + 128],
                                    jnp.broadcast_to(lrecv[g, pl.ds(2 * (2 * h + e) + k, 1), :], (8, 128)).astype(jnp.int32),
                                    axis=1,
                                )
                                for e in range(2)
                            ],
                            axis=1,
                        )
                        force = force + K_SPRING * (chosen - shift)
                    pull[i] = force
                floor = jnp.floor(position)
                above = position - floor
                below = 1.0 - above
                under = spanned(floor, 2)
                at_next, at_floor = ahead == under, depth == under
                nothing = jnp.zeros((128, 256), bf16)
                below_rest = below - below.astype(bf16).astype(f32)
                above_rest = above - above.astype(bf16).astype(f32)
                highs = jnp.where(at_next, spanned(above, 2), nothing)
                lows = jnp.where(at_next, spanned(above_rest, 2), nothing)
                pz[0:128, at] = jnp.where(at_floor, spanned(below, 2), highs)
                pz[128:256, at] = jnp.where(at_floor, spanned(below_rest, 2), lows)
            else:
                force = pull[i]
            wx = jnp.maximum(0.0, 1.0 - jnp.abs(position[0:1, :] - cell))
            wy = jnp.maximum(0.0, 1.0 - jnp.abs(position[1:2, :] - cell))
            full = jnp.concatenate([wx[x : x + 1, :] * wy for x in xs], axis=0)
            plane[0:size, at] = full
            for k in range(3):
                term = force[k : k + 1, :] * full
                high = term.astype(bf16)
                terms[k * size : k * size + size, at] = high
                terms[n + k * size : n + k * size + size, at] = (term - high.astype(f32)).astype(bf16)

        def gather(at):
            product = lax.dot_general(
                terms[0 : 2 * n, at], pz[:, at], (((1,), (1,)), ((), ())), preferred_element_type=f32
            )
            return product[0:n, 0:128] + (product[0:n, 128:256] + product[n : 2 * n, 0:128])

        total = None
        for turn in range(nx):
            if step == 0 and turn:
                arrive(*places, origins[turn])
            for h in range(cap // 2):
                one(turn, h)
            if step == 0:
                part = gather(pl.ds(turn * (cap * 128), cap * 128))
                total = part if total is None else total + part
        if step > 0:
            for h in range(4):
                part = gather(pl.ds(h * slots * 32, slots * 32))
                total = part if total is None else total + part
        for k in range(3):
            for i, x in enumerate(xs):
                gfield[k, x] = total[k * size + i * 8 : k * size + i * 8 + 8]

    def sample(xs, vsplit, plane):
        size = len(xs) * 8
        n = 3 * size
        v = jnp.concatenate([vfield[k, x] for k in range(3) for x in xs], axis=0)
        high = v.astype(jnp.bfloat16)
        low = (v - high.astype(jnp.float32)).astype(jnp.bfloat16)
        vsplit[0:n, 0:128] = high
        vsplit[0:n, 128:256] = high
        vsplit[n : 2 * n, 0:128] = low
        vsplit[n : 2 * n, 128:256] = low
        for i in range(slots * 128 // WIDE):
            at = pl.ds(i * WIDE, WIDE)
            product = jnp.dot(vsplit[0 : 2 * n], pz[:, at], preferred_element_type=jnp.float32)
            full = plane[0:size, at]
            for k in range(3):
                part = product[k * size : k * size + size] + product[n + k * size : n + k * size + size]
                moved = jnp.sum(part * full, axis=0, keepdims=True)
                for h in range(WIDE // 256):
                    pair = i * (WIDE // 256) + h
                    disp[pair, k : k + 1, :] = (
                        disp[pair, k : k + 1, :] + moved[:, h * 256 : h * 256 + 256]
                    )

    def first(x, packed):
        f = [pop[q, x] for q in range(19)]
        density, momentum = moments(f)
        mom[0, x] = density
        for k in range(3):
            mom[k + 1, x] = momentum[k]
        values = collide(f, density, momentum, None, solid[x] == 1)
        emit(0, x, values)
        return rim(0, x, values, packed)

    def coupled(step):
        def body(x, packed):
            f = [outf[q, x] for q in range(19)]
            values = collide(
                f, mom[0, x], [mom[k, x] for k in range(1, 4)],
                [gfield[k, x] for k in range(3)], solid[x] == 1,
            )
            emit(step, x, values)
            return rim(step, x, values, packed)

        return body

    def driven(x, carry):
        f = [pop[q, x] for q in range(19)]
        values = collide(
            f, mom[0, x], [mom[k, x] for k in range(1, 4)], [gfield[k, x] for k in range(3)],
            solid[x] == 1,
        )
        emit(0, x, values)
        return carry

    def moving(step):
        def body(x, carry):
            stream(step, x)
            return carry

        return body

    for copy in rims:
        copy.wait()
    packed = over_edges(first, jnp.zeros((8, 128), jnp.float32))
    zsend[0, 0] = packed
    x_halos = [halo_x(0)]
    core.wait()
    zsend[0, 1] = over_middle(first, packed)
    yz_halos = [halo_yz(0)]
    link_copies = exchange(*tethers)
    spread(0, inner, True, mid_terms, mid_plane)
    lax.fori_loop(2, cx - 2, driven, 0, unroll=cx - 4)

    for step in range(STEPS):
        last = step == STEPS - 1
        for copy in yz_halos[step]:
            copy.wait_recv()
        combine(step, False)
        over_middle(moving(step), 0)
        sample(inner if step == 0 else middle, vmid, mid_plane)
        if step == 0:
            for g in peers[::-1]:
                arrive(*tethers, g)
            spread(1, edges, True, edge_terms, edge_plane)
        for copy in x_halos[step]:
            copy.wait_recv()
        combine(step, True)
        over_edges(moving(step), 0)
        if step > 0:
            sample(edges, vedge, edge_plane)
        if last:
            break
        if step > 0:
            spread(step + 1, edges, True, edge_terms, edge_plane)
        packed = over_edges(coupled(step + 1), jnp.zeros((8, 128), jnp.float32))
        zsend[step + 1, 0] = packed
        for copy in x_halos[step]:
            copy.wait_send()
        x_halos.append(halo_x(step + 1))
        spread(step + 1, middle, False, mid_terms, mid_plane)
        zsend[step + 1, 1] = over_middle(coupled(step + 1), packed)
        for copy in yz_halos[step]:
            copy.wait_send()
        yz_halos.append(halo_yz(step + 1))

    for copy in place_copies:
        copy.wait_send()
    for c in range(slots):
        h = (c % 2) * 128
        at = 3 * (c % cap)
        dsend[origins[c // cap], at : at + 3, :] = disp[c // 2, 0:3, h : h + 128]
    back_copies = exchange(*returns)
    for copies in [link_copies, x_halos[-1], yz_halos[-1]]:
        for copy in copies:
            copy.wait_send()
    for g in peers[::-1]:
        arrive(*returns, g)
    tiles = [jnp.zeros((3, 128), jnp.float32) for b in range(blocks)]
    for c in range(slots):
        at = 3 * (c % cap)
        came = dback[c // cap, at : at + 3, :]
        tiles = [jnp.where(where_to[b, 0:3, :] == c, came, tiles[b]) for b in range(blocks)]
    for b in range(blocks):
        for k in range(3):
            outs[k, b : b + 1, :] = tiles[b][k : k + 1, :]
    for copy in back_copies:
        copy.wait_send()


def flush(new, shift, new_out, shift_out, a_sem, b_sem):
    a = pltpu.make_async_copy(new, new_out, a_sem)
    b = pltpu.make_async_copy(shift, shift_out, b_sem)
    a.start()
    b.start()
    a.wait()
    b.wait()


def shards(sizes, populations, solid, marker_pos, anchor_offset, links, patch_col):
    nx, ny, nz, blocks, cap, cx = sizes
    slots = nx * cap
    f32 = jnp.float32
    tile = (8, 128)
    mid = 8 * (cx - 2)
    padded = lambda rows: -(-rows // 8) * 8
    dma = pltpu.SemaphoreType.DMA
    new, shift = pl.pallas_call(
        functools.partial(kernel, sizes),
        out_shape=(
            pltpu.VMEM(populations.shape, f32),
            pltpu.VMEM((3, blocks, 128), f32),
        ),
        in_specs=[pl.BlockSpec(memory_space=pltpu.HBM)] * 6,
        scratch_shapes=[
            pltpu.VMEM(populations.shape, f32),
            pltpu.VMEM(solid.shape, jnp.int32),
            pltpu.VMEM((3, blocks, 128), f32),
            pltpu.VMEM((3, blocks, 128), f32),
            pltpu.VMEM(links.shape, jnp.int32),
            pltpu.VMEM((1, blocks), jnp.int32),
            pltpu.VMEM((STEPS, 19, cx + 2) + tile, f32),
            pltpu.VMEM((STEPS, 2, 5) + tile, f32),
            pltpu.VMEM((STEPS, 2, 5, 16, 128), f32),
            pltpu.VMEM((STEPS, 2) + tile, f32),
            pltpu.VMEM((STEPS, 5) + tile, f32),
            pltpu.VMEM(tile, f32),
            pltpu.VMEM((4, cx) + tile, f32),
            pltpu.VMEM((3, cx) + tile, f32),
            pltpu.VMEM((3, cx) + tile, f32),
            pltpu.VMEM((96, 256), jnp.bfloat16),
            pltpu.VMEM((6 * mid, 256), jnp.bfloat16),
            pltpu.VMEM((slots // 2, 8, 256), f32),
            pltpu.VMEM((nx, padded(6 * cap), 128), f32),
            pltpu.VMEM((nx, padded(6 * cap + 2), 128), f32),
            pltpu.VMEM((nx, padded(2 * cap), 128), f32),
            pltpu.VMEM((nx, padded(2 * cap), 128), f32),
            pltpu.VMEM((slots // 2, 8, 256), f32),
            pltpu.VMEM((nx, padded(3 * cap), 128), f32),
            pltpu.VMEM((nx, padded(3 * cap), 128), f32),
            pltpu.VMEM((blocks,) + tile, jnp.int32),
            pltpu.VMEM((96, slots * 128), jnp.bfloat16),
            pltpu.VMEM((6 * mid, slots * 128), jnp.bfloat16),
            pltpu.VMEM((256, slots * 128), jnp.bfloat16),
            pltpu.VMEM((16, slots * 128), f32),
            pltpu.VMEM((mid, slots * 128), f32),
            dma((2, nx)), dma((nx,)), dma((nx,)), dma((nx,)),
            dma((13,)), dma((2, 13)),
        ],
        compiler_params=pltpu.CompilerParams(
            collective_id=0, has_side_effects=True, vmem_limit_bytes=62 * 1024 * 1024
        ),
    )(
        populations,
        solid,
        jnp.transpose(marker_pos, (1, 0, 2)),
        jnp.transpose(anchor_offset, (1, 0, 2)),
        links,
        patch_col.T,
    )
    new, shift = pl.pallas_call(
        flush,
        out_shape=(
            jax.ShapeDtypeStruct(populations.shape, f32),
            jax.ShapeDtypeStruct((3, blocks, 128), f32),
        ),
        in_specs=[pl.BlockSpec(memory_space=pltpu.VMEM)] * 2,
        out_specs=(pl.BlockSpec(memory_space=pltpu.HBM),) * 2,
        scratch_shapes=[dma, dma],
    )(pltpu.with_memory_space_constraint(new, pltpu.VMEM), pltpu.with_memory_space_constraint(shift, pltpu.VMEM))
    return new, jnp.transpose(shift, (1, 0, 2))


def solution(mesh):
    placed = (
        P(None, "gx", "gy", "gz"),
        P("gx", "gy", "gz"),
        P(("gx", "gy", "gz"), None, None),
        P(("gx", "gy", "gz"), None, None),
        P(("gx", "gy", "gz"), None, None),
        P(("gx", "gy", "gz"), None),
    )

    def whole(populations, solid, marker_pos, anchor_offset, links, patch_col):
        nx, ny, nz = (mesh.shape[name] for name in ("gx", "gy", "gz"))
        blocks = marker_pos.shape[0] // (nx * ny * nz)
        cap = max(2, 2 * blocks // nx)
        sizes = (nx, ny, nz, blocks, cap, populations.shape[1] // nx)
        return jax.shard_map(
            functools.partial(shards, sizes),
            mesh=mesh,
            in_specs=placed,
            out_specs=(P(None, "gx", "gy", "gz"), P(("gx", "gy", "gz"), None, None)),
            check_vma=False,
        )(populations, solid, marker_pos, anchor_offset, links, patch_col)

    return whole
```
